512 devices in a mesh: view: 32 (over y, x, core), tile: 16 (over z).
Axes of the slice: x: 4, y: 4, z: 16, core: 2. Of those that a mesh axis runs over, the one named last changes fastest.
Arguments:
- centers: bfloat16 [384, 2, 128], P('tile'), may hold values from 4 to 28
- log_scales: bfloat16 [384, 2, 128], P('tile'), may hold values from -4 to -1.5
- correlation: bfloat16 [384, 128], P('tile'), may hold values from -0.59765625 to 0.59765625
- opacity_logit: bfloat16 [384, 128], P('tile'), may hold values from -6.5 to -2
- features: bfloat16 [384, 128, 128], P('tile'), may hold values from -16 to 16
- view_offset: float32 [32, 2], P('view'), may hold values from -3 to 3
- block_list: int32 [32, 32, 8], P('view', 'tile'), may hold values from 0 to 383, as said below
- pad_count: int32 [32, 32], P('view', 'tile'), may hold values from 0 to 7, as said below
- block_home: int32 [384], replicated, may hold values from 0 to 383, as said below
- image_grad: bfloat16 [32, 32, 1024, 128], P('view', 'tile'), may hold values from -6 to 6
Outputs:
- image: bfloat16 [32, 32, 1024, 128], P('view', 'tile')
- grad_centers: float32 [384, 2, 128], P('tile')
- grad_log_scales: float32 [384, 2, 128], P('tile')
- grad_correlation: float32 [384, 128], P('tile')
- grad_opacity: float32 [384, 128], P('tile')
- grad_features: float32 [384, 128, 128], P('tile')
The draws below stay inside these ranges and needn't reach their ends.
Inputs may be any that keep to these rules, and one draw needn't show every extreme that they name: `block_list`: the 2 lists of one view on one index of tile name at most 2 entries whose blocks lie in one shard of 24 rows (through block_home), padded entries included; in every such list set some shard is named exactly 2 times. Padded entries hold valid ids. `pad_count`: the first tile of every view has no padding. `block_home`: A permutation of the block ids.
All inputs are finite; a program needn't handle non-finite values.
Results may differ from the reference program's by a relative error of at most 0.0055.
Values may be sent and summed in bfloat16 or wider, within the bound.
No kernel may reach another device: no remote copies, remote signals or barrier semaphores. Data moves between devices by JAX's collectives and lax.ppermute only.
A program may use at most 64 MiB of HBM per device.

```python
import jax
import jax.numpy as jnp
from jax import lax

F = 128
BLOCK = 128
TILE_W = 32
MAXB = 8
TILES_DEV = 2
BLK_DEV = 24
VIEWS = 32
TILES = 32
NBLK_ALL = 384
PIX = 1024
CAP = 2
N_TILE = 16


def layout_tables(key):
    base_key = jax.random.fold_in(key, 7)
    home_key, owner_key, order_key, start_key, padding_key = jax.random.split(base_key, 5)
    home_table = jax.random.permutation(home_key, NBLK_ALL).astype(jnp.int32)
    inverse_table = jnp.argsort(home_table, stable=True).astype(jnp.int32)
    device_count = VIEWS * N_TILE
    slot_count = TILES_DEV * MAXB
    owner_perms = jax.vmap(lambda one_key: jax.random.permutation(one_key, N_TILE))(jax.random.split(owner_key, device_count)).astype(jnp.int32)
    slot_order = jax.vmap(lambda one_key: jax.random.permutation(one_key, slot_count))(jax.random.split(order_key, device_count)).astype(jnp.int32)
    owner_of = jnp.take_along_axis(owner_perms, slot_order // CAP, axis=1)
    starts = jax.random.randint(start_key, (device_count, N_TILE), 0, BLK_DEV).astype(jnp.int32)
    local_slot = (jnp.take_along_axis(starts, owner_of, axis=1) + slot_order % CAP) % BLK_DEV
    storage = owner_of * BLK_DEV + local_slot
    block_ids = jnp.take(inverse_table, storage.reshape(-1)).reshape(VIEWS, TILES, MAXB).astype(jnp.int32)
    padding = jax.random.randint(padding_key, (VIEWS, TILES), 0, MAXB).astype(jnp.int32)
    padding = padding.at[:, 0].set(0)
    return (home_table, block_ids, padding)


def draw_block_list(key, part):
    return layout_tables(key)[1]


def draw_pad_count(key, part):
    return layout_tables(key)[2]


def draw_block_home(key, part):
    return layout_tables(key)[0]


def block_levels(rng, dims, pieces, smallest, top_value):
    gain = 1.0
    for axis_at, shards_of in pieces:
        draws = jax.random.uniform(jax.random.fold_in(jax.random.fold_in(rng, 6), axis_at), (shards_of,), jnp.float32, smallest / len(pieces), top_value / len(pieces))
        gain = gain * jnp.repeat(jnp.exp(draws), dims[axis_at] // shards_of).reshape((-1,) + (1,) * (len(dims) - 1 - axis_at))
    return gain


def gaussian(own_key, shape, width, limit, shards=(), kind=jnp.bfloat16):
    array = width * jax.random.normal(own_key, shape, jnp.float32)
    if shards:
        array = array * block_levels(own_key, shape, shards, -0.22, 0.18)
    return jnp.clip(array, -limit, limit).astype(kind)


def setup_inputs(seed: int = 0) -> dict:
    keys = jax.random.split(jax.random.key(seed), 11)
    return {
        "centers": jnp.clip(4.0 + 24.0 * jax.random.uniform(keys[0], (NBLK_ALL, 2, BLOCK), jnp.float32) ** block_levels(keys[0], (NBLK_ALL, 2, BLOCK), ((0, 16),), -0.2, 0.2), 4.0, 28.0).astype(jnp.bfloat16),
        "log_scales": jnp.clip(-4.0 + 2.5 * jax.random.uniform(keys[1], (NBLK_ALL, 2, BLOCK), jnp.float32) ** block_levels(keys[1], (NBLK_ALL, 2, BLOCK), ((0, 16),), -0.2, 0.2), -4.0, -1.5).astype(jnp.bfloat16),
        "correlation": jnp.clip(jax.random.uniform(keys[2], (NBLK_ALL, BLOCK), jnp.float32, -0.59765625, 0.59765625) * block_levels(keys[2], (NBLK_ALL, BLOCK), ((0, 16),), -0.4, 0.0), -0.59765625, 0.59765625).astype(jnp.bfloat16),
        "opacity_logit": jnp.clip(-6.5 + 4.5 * jax.random.uniform(keys[3], (NBLK_ALL, BLOCK), jnp.float32) ** block_levels(keys[3], (NBLK_ALL, BLOCK), ((0, 16),), -0.2, 0.2), -6.5, -2.0).astype(jnp.bfloat16),
        "features": gaussian(keys[4], (NBLK_ALL, BLOCK, F), 4.0, 16.0, ((0, 16),)),
        "view_offset": jnp.clip(jax.random.uniform(keys[5], (VIEWS, 2), jnp.float32, -3.0, 3.0) * block_levels(keys[5], (VIEWS, 2), ((0, 32),), -0.4, 0.0), -3.0, 3.0),
        "block_list": draw_block_list(jax.random.fold_in(keys[10], 71), 0),
        "pad_count": draw_pad_count(jax.random.fold_in(keys[10], 71), 0),
        "block_home": draw_block_home(jax.random.fold_in(keys[10], 71), 0),
        "image_grad": gaussian(keys[9], (VIEWS, TILES, PIX, F), 1.0, 6.0, ((0, 32), (1, 16))),
    }


def pixel_grid():
    pixel_index = jnp.arange(TILE_W * TILE_W, dtype=jnp.int32)
    across = (pixel_index % TILE_W).astype(jnp.float32) + 0.5
    downward = (pixel_index // TILE_W).astype(jnp.float32) + 0.5
    return (across, downward)

def render_tile(tensors, alive_mask, offset):
    across, downward = pixel_grid()
    feature_width = tensors[4].shape[-1]

    def block_step(running, block_data):
        log_trans, colors = running
        center, log_scale, correl, opacity, feature, alive_flag = block_data
        delta_x = across[:, None] - (center[0] + offset[0])[None, :]
        delta_y = downward[:, None] - (center[1] + offset[1])[None, :]
        coef_a = jnp.exp(log_scale[0])
        coef_c = jnp.exp(log_scale[1])
        coef_b = correl * jnp.sqrt(coef_a * coef_c)
        quadric = coef_a[None, :] * delta_x * delta_x + 2.0 * coef_b[None, :] * delta_x * delta_y + coef_c[None, :] * delta_y * delta_y
        alphas = jax.nn.sigmoid(opacity)[None, :] * jnp.exp(-0.5 * quadric) * alive_flag
        log_keep = jnp.log1p(-alphas)
        before = jnp.cumsum(log_keep, axis=1) - log_keep
        weight = (alphas * jnp.exp(log_trans[:, None] + before)).astype(jnp.bfloat16)
        colors = colors + jnp.dot(weight, feature.astype(jnp.bfloat16), preferred_element_type=jnp.float32)
        log_trans = log_trans + lax.optimization_barrier(jnp.sum(log_keep, axis=1))
        return ((log_trans, colors), None)
    start_state = (jnp.zeros((across.shape[0],), jnp.float32), jnp.zeros((across.shape[0], feature_width), jnp.float32))
    (log_trans, colors), unused = lax.scan(jax.checkpoint(block_step), start_state, tuple(tensors) + (alive_mask,))
    return colors

def reference(centers, log_scales, correlation, opacity_logit, features, view_offset, block_list, pad_count, block_home, image_grad):
    flat_lists = block_list.reshape(VIEWS * TILES, MAXB)
    flat_pads = pad_count.reshape(VIEWS * TILES)
    flat_grad = image_grad.reshape(VIEWS * TILES, PIX, F)
    view_of = jnp.arange(VIEWS * TILES, dtype=jnp.int32) // TILES
    params = (centers, log_scales, correlation, opacity_logit, features)
    zero_sums = tuple((jnp.zeros(array_in.shape, jnp.float32) for array_in in params))

    def per_tile(totals, item_data):
        block_ids, pad_here, cotangent, view_index = item_data
        tile_rows = jnp.take(block_home, block_ids).astype(jnp.int32)
        inputs = tuple((jnp.take(array_in, tile_rows, axis=0).astype(jnp.float32) for array_in in params))
        alive_mask = (jnp.arange(MAXB, dtype=jnp.int32) < MAXB - pad_here).astype(jnp.float32)
        offset = view_offset[view_index]
        colors, pullback = jax.vjp(lambda *tensors: render_tile(tensors, alive_mask, offset), *inputs)
        grad_set = pullback(cotangent.astype(jnp.float32))
        totals = tuple((total_in.at[tile_rows].add(grad_in.astype(jnp.float32)) for total_in, grad_in in zip(totals, grad_set)))
        return (totals, colors.astype(jnp.bfloat16))
    totals, images = lax.scan(per_tile, zero_sums, (flat_lists, flat_pads, flat_grad, view_of))
    return (images.reshape(VIEWS, TILES, PIX, F), totals[0], totals[1], totals[2], totals[3], totals[4])
```

```python
import functools

import jax
import jax.numpy as jnp
from jax import lax
from jax.experimental import pallas as pl
from jax.experimental.pallas import tpu as pltpu
from jax.sharding import PartitionSpec as P

TILE_W = 32
PIX = 1024
F = 128
BLOCK = 128
LIST = 8
LANES = 128
WIDTH = 640
PARAMS = 8
LOG2E = 1.4426950408889634
CHUNKS = PIX // LANES
f32 = jnp.float32
bf16 = jnp.bfloat16

NN = (((1,), (0,)), ((), ()))
NT = (((1,), (1,)), ((), ()))
TN = (((0,), (0,)), ((), ()))


def dot(a, b, dims=NN, precision=None):
    return lax.dot_general(a, b, dims, precision=precision, preferred_element_type=f32)


def iota(shape, dim):
    return lax.broadcasted_iota(jnp.int32, shape, dim)


def lane_roll(x, shift):
    return pltpu.roll(x, shift % LANES, 1)


def split_pairs(x):
    kept = jnp.where(iota(x.shape, 1) < 32, x, 0.0)
    high = kept.astype(bf16).astype(f32)
    return high + lane_roll(kept - high, 32)


def fold_pairs(x):
    return x + lane_roll(x, -32)


def gather_kernel(ids_ref, table_ref, out_ref):
    rows = table_ref.shape[0]
    count = ids_ref.shape[1]
    hot = jnp.where(iota((rows, count), 0) == ids_ref[...], 1.0, 0.0).astype(bf16)
    out_ref[...] = dot(hot, table_ref[...], TN).astype(bf16)


def scatter_kernel(ids_ref, grads_ref, out_ref):
    rows = out_ref.shape[0]
    count = ids_ref.shape[1]
    hot = jnp.where(iota((rows, count), 0) == ids_ref[...], 1.0, 0.0).astype(bf16)
    total = dot(hot, grads_ref[...])
    out_ref[:, : 4 * F] = total[:, : 4 * F].astype(bf16)
    out_ref[:, 4 * F :] = split_pairs(fold_pairs(total[:, 4 * F :])).astype(bf16)


def sum_kernel(parts_ref, out_ref):
    total = parts_ref[0].astype(f32)
    for n in range(1, parts_ref.shape[0]):
        total = total + parts_ref[n].astype(f32)
    pairs = split_pairs(fold_pairs(total[:, 4 * F :]))
    total = jnp.concatenate([total[:, : 4 * F], pairs], axis=1).astype(bf16)
    for n in range(out_ref.shape[0]):
        out_ref[n] = total


def slot_permutation(slices, slots):
    count = slices * slots
    row, column = iota((count, count), 0), iota((count, count), 1)
    slot, place = row // slices, row % slices
    piece = (place % 8) * 4 + place // 8
    return jnp.where(column == piece * slots + slot, 1.0, 0.0).astype(bf16)


VISIT = [(t % 4) * 4 + t // 4 for t in range(16)]


def tile_kernel(
    pads_ref, offset_ref, blocks_ref, grad_ref, image_ref, sent_ref,
    rows, perm, basis, moments, feats_t, coefs, weights, weights_b, ratios, deltas, sums, trans, below, back,
):
    tile = pl.program_id(0)
    slots = 2 * LIST
    slices = 32

    @pl.when(tile == 0)
    def _():
        perm[...] = slot_permutation(slices, slots)
        rows[...] = dot(perm[...], blocks_ref[...]).astype(bf16)
        term, pixel = iota((LANES, PIX), 0), iota((LANES, PIX), 1)
        across, down = (pixel % TILE_W - 16).astype(f32), (pixel // TILE_W - 16).astype(f32)
        kind = jnp.where(term < 24, term % 8, 7)
        value = jnp.where(
            kind == 0, 1.0,
            jnp.where(kind == 1, across,
            jnp.where(kind == 2, down,
            jnp.where(kind == 3, across * across,
            jnp.where(kind == 4, across * down,
            jnp.where(kind == 5, down * down, 0.0))))))
        basis[...] = value.astype(bf16)
        term, lane = iota((8, LANES), 0), iota((8, LANES), 1)
        x, u = (lane % TILE_W - 16).astype(f32), (lane // TILE_W + 16).astype(f32)
        pick = lambda *values: functools.reduce(
            lambda rest, kv: jnp.where(term == kv[0], kv[1], rest), enumerate(values), jnp.zeros_like(x)
        )
        moments[:, :LANES] = pick(1.0, x, u, x * x, x * u, u * u)
        moments[:, LANES : 2 * LANES] = pick(0.0, 0.0, -4.0, 0.0, -4.0 * x, -8.0 * u - 16.0)
        moments[:, 2 * LANES :] = pick(0.0, 0.0, 0.0, 0.0, 0.0, 32.0)

    live = LIST - pads_ref[0, tile]
    shift_x, shift_y = offset_ref[0, 0] - 16.5, offset_ref[0, 1] - 16.5
    sub = iota((8, LANES), 0)

    lane = iota((BLOCK, LANES), 1)
    own = (lane % 4) == (iota((BLOCK, LANES), 0) // 32)
    rank = jnp.where(iota((8, LANES), 1) // 4 == iota((8, LANES), 0), 1.0, 0.0).astype(bf16)

    def parameters(k):
        at = pl.multiple_of((tile * LIST + k) * slices, slices)
        piece = rows[pl.ds(at, slices), 4 * F :]
        spread = jnp.where(own, jnp.concatenate([piece] * 4, axis=0).astype(f32), 0.0).astype(bf16)
        table = dot(rank, spread, NT)
        cx, cy = table[0:1] + shift_x, table[1:2] + shift_y
        a, c = jnp.exp(table[2:3]), jnp.exp(table[3:4])
        root = jnp.exp(0.5 * (table[2:3] + table[3:4]))
        return cx, cy, a, c, root, table[4:5] * root, table[5:6]

    def features(k):
        at = pl.multiple_of((tile * LIST + k) * slices, slices)
        return jnp.concatenate(
            [rows[pl.ds(at, slices), F * i : F * (i + 1)] for i in range(4)], axis=0
        )

    trans[...] = jnp.ones_like(trans)
    below[...] = jnp.zeros_like(below)

    def forward(k, unused):
        cx, cy, a, c, root, b, logit = parameters(k)
        h = -0.5 * LOG2E
        level = -LOG2E * jnp.log(1.0 + jnp.exp(-logit))
        terms = jnp.concatenate(
            [
                jnp.where(k < live, h * (a * cx * cx + 2.0 * b * cx * cy + c * cy * cy) + level, -1e30),
                (-2.0 * h) * (a * cx + b * cy),
                (-2.0 * h) * (b * cx + c * cy),
                h * a,
                (2.0 * h) * b,
                h * c,
                jnp.zeros((2, LANES), f32),
            ],
            axis=0,
        )
        high = terms.astype(bf16).astype(f32)
        middle = (terms - high).astype(bf16).astype(f32)
        low = terms - high - middle
        coef = jnp.concatenate([high, middle, low, jnp.zeros((LANES - 24, LANES), f32)], axis=0)
        coef = coef.T.astype(bf16)
        first = pl.multiple_of(k * BLOCK, BLOCK)
        feats_t[:, pl.ds(first, BLOCK)] = features(k).astype(f32).T.astype(bf16)
        for chunk in range(CHUNKS):
            columns = slice(chunk * LANES, (chunk + 1) * LANES)
            alpha = jnp.exp2(dot(coef, basis[:, columns]))
            keep = 1.0 - alpha
            ratios[pl.ds(first, BLOCK), columns] = alpha / keep
            before, run = [None] * 16, None
            for v in VISIT:
                before[v] = run
                piece = keep[8 * v : 8 * v + 8]
                run = piece if run is None else run * piece
            for step in (1, 2, 4):
                run = run * jnp.where(sub >= step, pltpu.roll(run, step, 0), 1.0)
            carry = trans[8 * chunk : 8 * chunk + 8]
            start = carry * jnp.where(sub >= 1, pltpu.roll(run, 1, 0), 1.0)
            trans[8 * chunk : 8 * chunk + 8] = carry * jnp.broadcast_to(run[7:8], (8, LANES))
            out = []
            for v in range(16):
                reach = start if before[v] is None else start * before[v]
                out.append(alpha[8 * v : 8 * v + 8] * reach)
            weight = jnp.concatenate(out, axis=0)
            weights[pl.ds(first, BLOCK), columns] = weight
            weights_b[pl.ds(first, BLOCK), columns] = weight.astype(bf16)
        return unused

    lax.fori_loop(0, LIST, forward, 0)

    image_ref[0, 0] = dot(feats_t[...], weights_b[...]).T.astype(bf16)

    def backward(step, unused):
        k = LIST - 1 - step
        first = pl.multiple_of(k * BLOCK, BLOCK)
        feats = features(k)
        for chunk in range(CHUNKS):
            columns = slice(chunk * LANES, (chunk + 1) * LANES)
            slope = dot(feats, grad_ref[0, 0, columns, :], NT)
            gain = slope * weights[pl.ds(first, BLOCK), columns]
            after, run = [None] * 16, None
            for v in VISIT[::-1]:
                after[v] = run
                piece = gain[8 * v : 8 * v + 8]
                run = piece if run is None else run + piece
            for shift in (1, 2, 4):
                run = run + jnp.where(sub < 8 - shift, pltpu.roll(run, 8 - shift, 0), 0.0)
            carry = below[8 * chunk : 8 * chunk + 8]
            start = carry + jnp.where(sub < 7, pltpu.roll(run, 7, 0), 0.0)
            below[8 * chunk : 8 * chunk + 8] = carry + jnp.broadcast_to(run[0:1], (8, LANES))
            out = []
            for v in range(16):
                rest = start if after[v] is None else start + after[v]
                ratio = ratios[pl.ds(first + 8 * v, 8), columns]
                out.append(gain[8 * v : 8 * v + 8] - rest * ratio)
            deltas[:, columns] = jnp.concatenate(out, axis=0)
        for v in range(16):
            once = twice = thrice = None
            for chunk in range(CHUNKS):
                piece = deltas[8 * v : 8 * v + 8, chunk * LANES : (chunk + 1) * LANES]
                once = piece if once is None else once + piece
                twice = once if twice is None else twice + once
                thrice = twice if thrice is None else thrice + twice
            sums[8 * v : 8 * v + 8, :LANES] = once
            sums[8 * v : 8 * v + 8, LANES : 2 * LANES] = twice
            sums[8 * v : 8 * v + 8, 2 * LANES :] = thrice
        table = dot(moments[...], sums[...], NT, lax.Precision.HIGHEST)
        cx, cy, a, c, root, b, logit = parameters(k)
        m0, mx, my, mxx, mxy, myy = (table[n : n + 1] for n in range(6))
        dx, dy = mx - cx * m0, my - cy * m0
        dxx = mxx - 2.0 * cx * mx + cx * cx * m0
        dxy = mxy - cx * my - cy * mx + cx * cy * m0
        dyy = myy - 2.0 * cy * my + cy * cy * m0
        grads = jnp.concatenate(
            [
                a * dx + b * dy,
                b * dx + c * dy,
                -0.5 * (a * dxx + b * dxy),
                -0.5 * (c * dyy + b * dxy),
                -root * dxy,
                m0 / (1.0 + jnp.exp(logit)),
                jnp.zeros((2, LANES), f32),
            ],
            axis=0,
        )
        high = grads.astype(bf16).astype(f32)
        low = grads - high
        group = iota((8, LANES), 1) // 32
        both = [jnp.where(group == i, part, 0.0) for part in (high, low) for i in range(4)]
        both.append(jnp.zeros((LANES - 64, LANES), f32))
        turned = jnp.concatenate(both, axis=0).T
        packed = turned[0:32] + turned[32:64] + turned[64:96] + turned[96:128]
        pulled = dot(weights_b[pl.ds(first, BLOCK), :], grad_ref[0, 0])
        at = pl.multiple_of((tile * LIST + k) * slices, slices)
        for i in range(4):
            back[pl.ds(at, slices), F * i : F * (i + 1)] = pulled[32 * i : 32 * i + 32].astype(bf16)
        back[pl.ds(at, slices), 4 * F :] = packed.astype(bf16)
        return unused

    lax.fori_loop(0, LIST, backward, 0)

    @pl.when(tile == 1)
    def _():
        sent_ref[...] = dot(perm[...], back[...], TN).astype(bf16)


def in_vmem(kernel, out_shape, *args):
    spec = pl.BlockSpec(memory_space=pltpu.VMEM)
    return pl.pallas_call(
        kernel, out_shape=out_shape, in_specs=[spec] * len(args), out_specs=spec
    )(*args)


def tile_call(pads, offset, blocks, grad):
    count = blocks.shape[0]
    smem = pl.BlockSpec(memory_space=pltpu.SMEM)
    whole = pl.BlockSpec((count, WIDTH), lambda t: (0, 0))
    image = pl.BlockSpec((1, 1, PIX, F), lambda t: (0, t, 0, 0))
    every = LIST * BLOCK
    return pl.pallas_call(
        tile_kernel,
        grid=(2,),
        out_shape=(
            jax.ShapeDtypeStruct(grad.shape, bf16),
            jax.ShapeDtypeStruct((count, WIDTH), bf16),
        ),
        in_specs=[smem, smem, whole, image],
        out_specs=(image, whole),
        scratch_shapes=[
            pltpu.VMEM((count, WIDTH), bf16),
            pltpu.VMEM((count, count), bf16),
            pltpu.VMEM((LANES, PIX), bf16),
            pltpu.VMEM((8, 3 * LANES), f32),
            pltpu.VMEM((F, every), bf16),
            pltpu.VMEM((8, LANES), f32),
            pltpu.VMEM((every, PIX), f32),
            pltpu.VMEM((every, PIX), bf16),
            pltpu.VMEM((every, PIX), f32),
            pltpu.VMEM((BLOCK, PIX), f32),
            pltpu.VMEM((BLOCK, 3 * LANES), f32),
            pltpu.VMEM((8 * CHUNKS, LANES), f32),
            pltpu.VMEM((8 * CHUNKS, LANES), f32),
            pltpu.VMEM((count, WIDTH), bf16),
        ],
        compiler_params=pltpu.CompilerParams(vmem_limit_bytes=48 * 1024 * 1024),
    )(pads, offset, blocks, grad)


def shards(
    centers,
    log_scales,
    correlation,
    opacity_logit,
    features,
    view_offset,
    block_list,
    pad_count,
    block_home,
    image_grad,
):
    views, tiles = lax.axis_size("view"), lax.axis_size("tile")
    held = centers.shape[0]
    total = held * tiles
    part = BLOCK // views
    view = lax.axis_index("view")

    def exchange(x, axis):
        return lax.all_to_all(x, axis, split_axis=0, concat_axis=0, tiled=True)

    rows = jnp.take(block_home, block_list.reshape(-1))
    slots = rows.shape[0]
    ids = exchange(jnp.broadcast_to(rows[None], (views, slots)), "view").reshape(1, -1)
    small = jnp.concatenate(
        [centers, log_scales, correlation[:, None], opacity_logit[:, None]], axis=1
    )
    small = lax.dynamic_slice_in_dim(small, view * part, part, axis=2).reshape(held, -1)
    mine = lax.dynamic_slice_in_dim(features, view * part, part, axis=1).reshape(held, -1)
    fill = jnp.zeros((held, WIDTH - part * F - small.shape[1]), bf16)
    slab = jnp.concatenate([mine, small, fill], axis=1)
    slab = jnp.broadcast_to(slab[None], (tiles, held, WIDTH)).reshape(total, WIDTH)
    table = exchange(slab, "tile")
    wanted = in_vmem(gather_kernel, jax.ShapeDtypeStruct((views * slots, WIDTH), bf16), ids, table)
    blocks = exchange(wanted, "view")

    image, sent = tile_call(pad_count, view_offset, blocks, image_grad)

    came = exchange(sent, "view")
    partial = in_vmem(scatter_kernel, jax.ShapeDtypeStruct((total, WIDTH), bf16), ids, came)
    partial = exchange(partial, "tile").reshape(tiles, held, WIDTH)
    slab = in_vmem(sum_kernel, jax.ShapeDtypeStruct((views, held, WIDTH), bf16), partial)
    slab = exchange(slab, "view")

    grads = slab[:, :, : part * F].reshape(views, held, part, F).transpose(1, 0, 2, 3)
    grad_features = grads.reshape(held, BLOCK, F).astype(f32)
    pairs = slab[:, :, part * F :].astype(f32)
    pairs = pairs[:, :, : part * PARAMS] + pairs[:, :, part * PARAMS : 2 * part * PARAMS]
    pairs = pairs.reshape(views, held, part, PARAMS).transpose(1, 3, 0, 2)
    pairs = pairs.reshape(held, PARAMS, BLOCK)
    return (image, pairs[:, 0:2], pairs[:, 2:4], pairs[:, 4], pairs[:, 5], grad_features)


def solution(mesh):
    in_specs = (
        P("tile", None, None),
        P("tile", None, None),
        P("tile", None),
        P("tile", None),
        P("tile", None, None),
        P("view", None),
        P("view", "tile", None),
        P("view", "tile"),
        P(),
        P("view", "tile", None, None),
    )
    out_specs = (
        P("view", "tile", None, None),
        P("tile", None, None),
        P("tile", None, None),
        P("tile", None),
        P("tile", None),
        P("tile", None, None),
    )
    return jax.shard_map(shards, mesh=mesh, in_specs=in_specs, out_specs=out_specs, check_vma=False)
```

```python
import functools

import jax
import jax.numpy as jnp
from jax import lax
from jax.experimental import pallas as pl
from jax.experimental.pallas import tpu as pltpu
from jax.sharding import PartitionSpec as P


TILE_W = 32
PIX = 1024
F = 128
BLOCK = 128
LIST = 8
LANES = 128
WIDTH = 640
LOG2E = 1.4426950408889634
CHUNKS = PIX // LANES
UNROLL = 2
f32 = jnp.float32
bf16 = jnp.bfloat16

NN = (((1,), (0,)), ((), ()))
NT = (((1,), (1,)), ((), ()))
TN = (((0,), (0,)), ((), ()))


def dot(a, b, dims=NN, precision=None):
    return lax.dot_general(a, b, dims, precision=precision, preferred_element_type=f32)


def iota(shape, dim):
    return lax.broadcasted_iota(jnp.int32, shape, dim)


def lane_roll(x, shift):
    return pltpu.roll(x, shift % LANES, 1)


def split_pairs(x):
    kept = jnp.where(iota(x.shape, 1) < 32, x, 0.0)
    high = kept.astype(bf16).astype(f32)
    return high + lane_roll(kept - high, 32)


def fold_pairs(x):
    return x + lane_roll(x, -32)


def gather_kernel(ids_ref, table_ref, out_ref):
    rows = table_ref.shape[0]
    count = ids_ref.shape[1]
    hot = jnp.where(iota((rows, count), 0) == ids_ref[...], 1.0, 0.0).astype(bf16)
    out_ref[...] = dot(hot, table_ref[...], TN).astype(bf16)


def scatter_kernel(ids_ref, grads_ref, out_ref):
    rows = out_ref.shape[0]
    count = ids_ref.shape[1]
    hot = jnp.where(iota((rows, count), 0) == ids_ref[...], 1.0, 0.0).astype(bf16)
    total = dot(hot, grads_ref[...])
    out_ref[:, : 4 * F] = total[:, : 4 * F].astype(bf16)
    out_ref[:, 4 * F :] = split_pairs(fold_pairs(total[:, 4 * F :])).astype(bf16)


def sum_kernel(parts_ref, out_ref):
    total = parts_ref[0].astype(f32)
    for n in range(1, parts_ref.shape[0]):
        total = total + parts_ref[n].astype(f32)
    pairs = split_pairs(fold_pairs(total[:, 4 * F :]))
    total = jnp.concatenate([total[:, : 4 * F], pairs], axis=1).astype(bf16)
    for n in range(out_ref.shape[0]):
        out_ref[n] = total


def slot_permutation(slices, slots):
    count = slices * slots
    row, column = iota((count, count), 0), iota((count, count), 1)
    slot, place = row // slices, row % slices
    piece = (place % 8) * 4 + place // 8
    return jnp.where(column == piece * slots + slot, 1.0, 0.0).astype(bf16)


VISIT = [(t % 4) * 4 + t // 4 for t in range(16)]
EVERY = LIST * BLOCK


def tile_kernel(
    pads_ref, offset_ref, blocks_ref, grad_ref, image_ref, sent_ref,
    rows, perm, basis, moments, feats, feats_t, coefs, weights, weights_b, ratios, deltas, sums, trans, below, back,
):
    tile = pl.program_id(0)
    slots = 2 * LIST
    slices = 32

    @pl.when(tile == 0)
    def _():
        perm[...] = slot_permutation(slices, slots)
        rows[...] = dot(perm[...], blocks_ref[...]).astype(bf16)
        term, pixel = iota((LANES, PIX), 0), iota((LANES, PIX), 1)
        across, down = (pixel % TILE_W - 16).astype(f32), (pixel // TILE_W - 16).astype(f32)
        kind = jnp.where(term < 24, term % 8, 7)
        value = jnp.where(
            kind == 0, 1.0,
            jnp.where(kind == 1, across,
            jnp.where(kind == 2, down,
            jnp.where(kind == 3, across * across,
            jnp.where(kind == 4, across * down,
            jnp.where(kind == 5, down * down, 0.0))))))
        basis[...] = value.astype(bf16)
        term, lane = iota((16, LANES), 0), iota((16, LANES), 1)
        x, y = (lane % TILE_W - 16).astype(f32), (lane // TILE_W).astype(f32)
        one = jnp.ones_like(x)
        pick = lambda first, *values: functools.reduce(
            lambda rest, kv: jnp.where(term == kv[0], kv[1], rest),
            enumerate(values, first), jnp.zeros_like(x),
        )
        moments[:, :LANES] = pick(0, one, x, y, x * x, x * y, y * y).astype(bf16)
        moments[:, LANES : 2 * LANES] = pick(6, one, x, y).astype(bf16)
        moments[:, 2 * LANES :] = pick(9, one).astype(bf16)

    live = LIST - pads_ref[0, tile]
    shift_x, shift_y = offset_ref[0, 0] - 16.5, offset_ref[0, 1] - 16.5
    sub = iota((8, LANES), 0)

    lane = iota((BLOCK, LANES), 1)
    own = (lane % 4) == (iota((BLOCK, LANES), 0) // 32)
    rank = jnp.where(iota((8, LANES), 1) // 4 == iota((8, LANES), 0), 1.0, 0.0).astype(bf16)
    spread = []
    for k in range(LIST):
        at = pl.multiple_of((tile * LIST + k) * slices, slices)
        piece = rows[pl.ds(at, slices), 4 * F :]
        piece = jnp.concatenate([piece] * 4, axis=0).astype(f32)
        spread.append(jnp.where(own, piece, 0.0).astype(bf16))
        feat = jnp.concatenate(
            [rows[pl.ds(at, slices), F * i : F * (i + 1)] for i in range(4)], axis=0
        )
        feats[BLOCK * k : BLOCK * (k + 1), :] = feat
        feats_t[:, BLOCK * k : BLOCK * (k + 1)] = feat.astype(f32).T.astype(bf16)
    table = dot(rank, jnp.concatenate(spread, axis=0), NT)
    cx, cy = table[0:1] + shift_x, table[1:2] + shift_y
    a, c = jnp.exp(table[2:3]), jnp.exp(table[3:4])
    root = jnp.exp(0.5 * (table[2:3] + table[3:4]))
    b, logit = table[4:5] * root, table[5:6]

    h = -0.5 * LOG2E
    level = -LOG2E * jnp.log(1.0 + jnp.exp(-logit))
    level = level + h * (a * cx * cx + 2.0 * b * cx * cy + c * cy * cy)
    terms = jnp.concatenate(
        [
            jnp.where(iota((1, EVERY), 1) // BLOCK < live, level, -1e30),
            (-2.0 * h) * (a * cx + b * cy),
            (-2.0 * h) * (b * cx + c * cy),
            h * a,
            (2.0 * h) * b,
            h * c,
            jnp.zeros((2, EVERY), f32),
        ],
        axis=0,
    )
    high = terms.astype(bf16).astype(f32)
    middle = (terms - high).astype(bf16).astype(f32)
    parts = [high, middle, terms - high - middle]
    for k in range(LIST):
        square = [part[:, BLOCK * k : BLOCK * (k + 1)] for part in parts]
        square = jnp.concatenate(square + [jnp.zeros((LANES - 24, LANES), f32)], axis=0)
        coefs[BLOCK * k : BLOCK * (k + 1), :] = square.T.astype(bf16)

    trans[...] = jnp.ones_like(trans)
    below[...] = jnp.zeros_like(below)

    def forward(k):
        first = pl.multiple_of(k * BLOCK, BLOCK)
        coef = coefs[pl.ds(first, BLOCK), :]
        for chunk in range(CHUNKS):
            columns = slice(chunk * LANES, (chunk + 1) * LANES)
            alpha = jnp.exp2(dot(coef, basis[:, columns]))
            keep = 1.0 - alpha
            ratios[pl.ds(first, BLOCK), columns] = alpha / keep
            before, run = [None] * 16, None
            for v in VISIT:
                before[v] = run
                piece = keep[8 * v : 8 * v + 8]
                run = piece if run is None else run * piece
            for step in (1, 2, 4):
                run = run * jnp.where(sub >= step, pltpu.roll(run, step, 0), 1.0)
            carry = trans[8 * chunk : 8 * chunk + 8]
            start = carry * jnp.where(sub >= 1, pltpu.roll(run, 1, 0), 1.0)
            trans[8 * chunk : 8 * chunk + 8] = carry * jnp.broadcast_to(run[7:8], (8, LANES))
            out = []
            for v in range(16):
                reach = start if before[v] is None else start * before[v]
                out.append(alpha[8 * v : 8 * v + 8] * reach)
            weight = jnp.concatenate(out, axis=0)
            weights[pl.ds(first, BLOCK), columns] = weight
            weights_b[pl.ds(first, BLOCK), columns] = weight.astype(bf16)

    def backward(k):
        first = pl.multiple_of(k * BLOCK, BLOCK)
        feat = feats[pl.ds(first, BLOCK), :]
        for chunk in range(CHUNKS):
            columns = slice(chunk * LANES, (chunk + 1) * LANES)
            slope = dot(feat, grad_ref[0, 0, columns, :], NT)
            gain = slope * weights[pl.ds(first, BLOCK), columns]
            after, run = [None] * 16, None
            for v in VISIT[::-1]:
                after[v] = run
                piece = gain[8 * v : 8 * v + 8]
                run = piece if run is None else run + piece
            for shift in (1, 2, 4):
                run = run + jnp.where(sub < 8 - shift, pltpu.roll(run, 8 - shift, 0), 0.0)
            carry = below[8 * chunk : 8 * chunk + 8]
            start = carry + jnp.where(sub < 7, pltpu.roll(run, 7, 0), 0.0)
            below[8 * chunk : 8 * chunk + 8] = carry + jnp.broadcast_to(run[0:1], (8, LANES))
            out = []
            for v in range(16):
                rest = start if after[v] is None else start + after[v]
                ratio = ratios[pl.ds(first + 8 * v, 8), columns]
                out.append(gain[8 * v : 8 * v + 8] - rest * ratio)
            deltas[:, columns] = jnp.concatenate(out, axis=0)
        for v in range(16):
            once = twice = thrice = None
            for chunk in range(CHUNKS):
                piece = deltas[8 * v : 8 * v + 8, chunk * LANES : (chunk + 1) * LANES]
                once = piece if once is None else once + piece
                twice = once if twice is None else twice + once
                thrice = twice if thrice is None else thrice + twice
            at = pl.ds(first + 8 * v, 8)
            sums[at, :LANES] = once
            sums[at, LANES : 2 * LANES] = twice
            sums[at, 2 * LANES :] = thrice

    def both(step, entry):
        for n in range(UNROLL):
            entry(step * UNROLL + n)

    lax.fori_loop(0, LIST // UNROLL, lambda step, u: (both(step, forward), u)[1], 0)
    image_ref[0, 0] = dot(feats_t[...], weights_b[...]).T.astype(bf16)
    lax.fori_loop(
        0, LIST // UNROLL, lambda step, u: (both(step, lambda n: backward(LIST - 1 - n)), u)[1], 0
    )

    pulled = dot(weights_b[...], grad_ref[0, 0]).astype(bf16)
    high = sums[...].astype(bf16)
    middle = (sums[...] - high.astype(f32)).astype(bf16)
    table = dot(moments[...], high, NT) + dot(moments[...], middle, NT)
    s, sx, sy, sxx, sxy, syy, t, tx, ty, w = (table[n : n + 1] for n in range(10))
    m0, mx, mxx = s, sx, sxx
    my = sy + 16.0 * s - 4.0 * t
    mxy = sxy + 16.0 * sx - 4.0 * tx
    myy = syy + 32.0 * sy + 256.0 * s - 8.0 * ty - 144.0 * t + 32.0 * w
    dx, dy = mx - cx * m0, my - cy * m0
    dxx = mxx - 2.0 * cx * mx + cx * cx * m0
    dxy = mxy - cx * my - cy * mx + cx * cy * m0
    dyy = myy - 2.0 * cy * my + cy * cy * m0
    grads = jnp.concatenate(
        [
            a * dx + b * dy,
            b * dx + c * dy,
            -0.5 * (a * dxx + b * dxy),
            -0.5 * (c * dyy + b * dxy),
            -root * dxy,
            m0 / (1.0 + jnp.exp(logit)),
            jnp.zeros((2, EVERY), f32),
        ],
        axis=0,
    )
    high = grads.astype(bf16).astype(f32)
    low = grads - high
    group = iota((8, LANES), 1) // 32
    for k in range(LIST):
        pair = [part[:, BLOCK * k : BLOCK * (k + 1)] for part in (high, low)]
        pair = [jnp.where(group == i, part, 0.0) for part in pair for i in range(4)]
        pair.append(jnp.zeros((LANES - 64, LANES), f32))
        turned = jnp.concatenate(pair, axis=0).T
        packed = turned[0:32] + turned[32:64] + turned[64:96] + turned[96:128]
        at = pl.multiple_of((tile * LIST + k) * slices, slices)
        for i in range(4):
            first = BLOCK * k + 32 * i
            back[pl.ds(at, slices), F * i : F * (i + 1)] = pulled[first : first + 32]
        back[pl.ds(at, slices), 4 * F :] = packed.astype(bf16)

    @pl.when(tile == 1)
    def _():
        sent_ref[...] = dot(perm[...], back[...], TN).astype(bf16)


def finish_kernel(slab_ref, centers_ref, scales_ref, corr_ref, opac_ref, feats_ref, wide, tall):
    slices, held = slab_ref.shape[0], slab_ref.shape[1]
    for n in range(slices):
        for i in range(5):
            wide[i, held * n : held * (n + 1), :] = slab_ref[n, :, F * i : F * (i + 1)].astype(f32)
    lane = iota((slices, LANES), 1)
    place = jnp.where(lane < 64, (lane % 32) // 8, -1)
    for n in range(held):
        at = pl.ds(n, slices, stride=held)
        small = wide[4, at, :]
        for i in range(4):
            feats_ref[n, pl.ds(i, slices, stride=4), :] = wide[i, at, :]
            tall[pl.ds(BLOCK * n + i, slices, stride=4), :] = jnp.where(place == i, small, 0.0)
    rank = jnp.where(iota((8, LANES), 1) % 8 == iota((8, LANES), 0), 1.0, 0.0).astype(bf16)
    table = dot(rank, tall[...].astype(bf16), NT)
    for n in range(held):
        own = table[:, BLOCK * n : BLOCK * (n + 1)]
        centers_ref[n] = own[0:2]
        scales_ref[n] = own[2:4]
        corr_ref[n : n + 1, :] = own[4:5]
        opac_ref[n : n + 1, :] = own[5:6]


def cut_kernel(view_ref, params_ref, feats_ref, out_ref):
    held = feats_ref.shape[0]
    view = view_ref[0]
    part = 4
    base = pl.multiple_of((view // 4) * 16, 16)
    near = feats_ref[:, pl.ds(base, 16), :].reshape(held * 16, F)
    row, column = iota((held, held * 16), 0), iota((held, held * 16), 1)
    cuts = []
    for i in range(part):
        hot = jnp.where(column == row * 16 + (view % 4) * part + i, 1.0, 0.0).astype(bf16)
        cuts.append(dot(hot, near))
    gauss, lane = iota((BLOCK, LANES), 0) - view * part, iota((BLOCK, LANES), 1)
    small = jnp.zeros((held, LANES), f32)
    for j in range(params_ref.shape[0]):
        chosen = (lane == gauss + part * j) & (gauss >= 0) & (gauss < part)
        small = small + dot(params_ref[j], jnp.where(chosen, 1.0, 0.0).astype(bf16))
    slab = jnp.concatenate(cuts + [small], axis=1).astype(bf16)
    for n in range(out_ref.shape[0]):
        out_ref[n] = slab


def in_vmem(kernel, shape, *args):
    spec = pl.BlockSpec(memory_space=pltpu.VMEM)
    return pl.pallas_call(
        kernel, out_shape=pltpu.VMEM(shape, bf16), in_specs=[spec] * len(args), out_specs=spec
    )(*args)


def tile_call(pads, offset, blocks, grad):
    count = blocks.shape[0]
    smem = pl.BlockSpec(memory_space=pltpu.SMEM)
    whole = pl.BlockSpec((count, WIDTH), lambda t: (0, 0))
    image = pl.BlockSpec((1, 1, PIX, F), lambda t: (0, t, 0, 0))
    return pl.pallas_call(
        tile_kernel,
        grid=(2,),
        out_shape=(
            jax.ShapeDtypeStruct(grad.shape, bf16),
            jax.ShapeDtypeStruct((count, WIDTH), bf16),
        ),
        in_specs=[smem, smem, whole, image],
        out_specs=(image, whole),
        scratch_shapes=[
            pltpu.VMEM((count, WIDTH), bf16),
            pltpu.VMEM((count, count), bf16),
            pltpu.VMEM((LANES, PIX), bf16),
            pltpu.VMEM((16, 3 * LANES), bf16),
            pltpu.VMEM((EVERY, F), bf16),
            pltpu.VMEM((F, EVERY), bf16),
            pltpu.VMEM((EVERY, LANES), bf16),
            pltpu.VMEM((EVERY, PIX), f32),
            pltpu.VMEM((EVERY, PIX), bf16),
            pltpu.VMEM((EVERY, PIX), f32),
            pltpu.VMEM((BLOCK, PIX), f32),
            pltpu.VMEM((EVERY, 3 * LANES), f32),
            pltpu.VMEM((8 * CHUNKS, LANES), f32),
            pltpu.VMEM((8 * CHUNKS, LANES), f32),
            pltpu.VMEM((count, WIDTH), bf16),
        ],
        compiler_params=pltpu.CompilerParams(vmem_limit_bytes=48 * 1024 * 1024),
    )(pads, offset, blocks, grad)


def shards(
    centers,
    log_scales,
    correlation,
    opacity_logit,
    features,
    view_offset,
    block_list,
    pad_count,
    block_home,
    image_grad,
):
    views, tiles = lax.axis_size("view"), lax.axis_size("tile")
    held = centers.shape[0]
    total = held * tiles
    view = lax.axis_index("view")

    def exchange(x, axis):
        return lax.all_to_all(x, axis, split_axis=0, concat_axis=0, tiled=True)

    params = jnp.stack(
        [centers[:, 0], centers[:, 1], log_scales[:, 0], log_scales[:, 1], correlation, opacity_logit]
    )
    spec = pl.BlockSpec(memory_space=pltpu.VMEM)
    slab = pl.pallas_call(
        cut_kernel,
        out_shape=jax.ShapeDtypeStruct((tiles, held, WIDTH), bf16),
        in_specs=[pl.BlockSpec(memory_space=pltpu.SMEM), spec, spec],
        out_specs=spec,
    )(view.reshape(1), params, features)
    table = exchange(slab, "tile")
    rows = jnp.take(block_home, block_list.reshape(-1))
    slots = rows.shape[0]
    asked = lax.all_gather(rows, "view")
    table, ids = table.reshape(total, WIDTH), asked.reshape(1, -1)
    wanted = in_vmem(gather_kernel, (views * slots, WIDTH), ids, table)
    blocks = exchange(wanted, "view")

    image, sent = tile_call(pad_count, view_offset, blocks, image_grad)

    came = exchange(sent, "view")
    partial = in_vmem(scatter_kernel, (total, WIDTH), ids, came)
    partial = exchange(partial, "tile").reshape(tiles, held, WIDTH)
    slab = in_vmem(sum_kernel, (views, held, WIDTH), partial)
    slab = exchange(slab, "view")

    shape = lambda *dims: jax.ShapeDtypeStruct(dims, f32)
    spec = pl.BlockSpec(memory_space=pltpu.VMEM)
    grads = pl.pallas_call(
        finish_kernel,
        out_shape=(
            shape(held, 2, BLOCK), shape(held, 2, BLOCK), shape(held, BLOCK), shape(held, BLOCK),
            shape(held, BLOCK, F),
        ),
        in_specs=[spec],
        out_specs=(spec,) * 5,
        scratch_shapes=[
            pltpu.VMEM((5, views * held, LANES), f32),
            pltpu.VMEM((held * BLOCK, LANES), f32),
        ],
    )(slab)
    return (image, *grads)


def solution(mesh):
    in_specs = (
        P("tile", None, None),
        P("tile", None, None),
        P("tile", None),
        P("tile", None),
        P("tile", None, None),
        P("view", None),
        P("view", "tile", None),
        P("view", "tile"),
        P(),
        P("view", "tile", None, None),
    )
    out_specs = (
        P("view", "tile", None, None),
        P("tile", None, None),
        P("tile", None, None),
        P("tile", None),
        P("tile", None),
        P("tile", None, None),
    )
    return jax.shard_map(shards, mesh=mesh, in_specs=in_specs, out_specs=out_specs, check_vma=False)
```

```python
import functools

import jax
import jax.numpy as jnp
from jax import lax
from jax.experimental import pallas as pl
from jax.experimental.pallas import tpu as pltpu
from jax.sharding import PartitionSpec as P


TILE_W = 32
PIX = 1024
F = 128
BLOCK = 128
LIST = 8
LANES = 128
WIDTH = 640
LOG2E = 1.4426950408889634
CHUNKS = PIX // LANES
UNROLL = 8
f32 = jnp.float32
bf16 = jnp.bfloat16

NN = (((1,), (0,)), ((), ()))
NT = (((1,), (1,)), ((), ()))
TN = (((0,), (0,)), ((), ()))


def dot(a, b, dims=NN, precision=None):
    return lax.dot_general(a, b, dims, precision=precision, preferred_element_type=f32)


def iota(shape, dim):
    return lax.broadcasted_iota(jnp.int32, shape, dim)


def lane_roll(x, shift):
    return pltpu.roll(x, shift % LANES, 1)


def split_pairs(x):
    kept = jnp.where(iota(x.shape, 1) < 32, x, 0.0)
    high = kept.astype(bf16).astype(f32)
    return high + lane_roll(kept - high, 32)


def fold_pairs(x):
    return x + lane_roll(x, -32)


def gather_kernel(ids_ref, table_ref, out_ref):
    rows = table_ref.shape[0]
    count = ids_ref.shape[1]
    hot = jnp.where(iota((rows, count), 0) == ids_ref[...], 1.0, 0.0).astype(bf16)
    out_ref[...] = dot(hot, table_ref[...], TN).astype(bf16)


def scatter_kernel(ids_ref, grads_ref, out_ref):
    rows = out_ref.shape[0]
    count = ids_ref.shape[1]
    hot = jnp.where(iota((rows, count), 0) == ids_ref[...], 1.0, 0.0).astype(bf16)
    total = dot(hot, grads_ref[...])
    out_ref[:, : 4 * F] = total[:, : 4 * F].astype(bf16)
    out_ref[:, 4 * F :] = split_pairs(fold_pairs(total[:, 4 * F :])).astype(bf16)


def sum_kernel(parts_ref, out_ref):
    total = parts_ref[0].astype(f32)
    for n in range(1, parts_ref.shape[0]):
        total = total + parts_ref[n].astype(f32)
    pairs = split_pairs(fold_pairs(total[:, 4 * F :]))
    total = jnp.concatenate([total[:, : 4 * F], pairs], axis=1).astype(bf16)
    for n in range(out_ref.shape[0]):
        out_ref[n] = total


def slot_permutation(slices, slots):
    count = slices * slots
    row, column = iota((count, count), 0), iota((count, count), 1)
    slot, place = row // slices, row % slices
    piece = (place % 8) * 4 + place // 8
    return jnp.where(column == piece * slots + slot, 1.0, 0.0).astype(bf16)


VISIT = [(t % 4) * 4 + t // 4 for t in range(16)]
EVERY = LIST * BLOCK


def tile_kernel(
    pads_ref, offset_ref, blocks_ref, grad_ref, image_ref, sent_ref,
    rows, perm, basis, moments, feats, feats_t, coefs, weights, weights_b, ratios, deltas, sums, trans, below, back,
):
    tile = pl.program_id(0)
    slots = 2 * LIST
    slices = 32

    @pl.when(tile == 0)
    def _():
        perm[...] = slot_permutation(slices, slots)
        rows[...] = dot(perm[...], blocks_ref[...]).astype(bf16)
        term, pixel = iota((LANES, PIX), 0), iota((LANES, PIX), 1)
        across, down = (pixel % TILE_W - 16).astype(f32), (pixel // TILE_W - 16).astype(f32)
        kind = jnp.where(term < 24, term % 8, 7)
        value = jnp.where(
            kind == 0, 1.0,
            jnp.where(kind == 1, across,
            jnp.where(kind == 2, down,
            jnp.where(kind == 3, across * across,
            jnp.where(kind == 4, across * down,
            jnp.where(kind == 5, down * down, 0.0))))))
        basis[...] = value.astype(bf16)
        term, lane = iota((16, LANES), 0), iota((16, LANES), 1)
        x, y = (lane % TILE_W - 16).astype(f32), (lane // TILE_W).astype(f32)
        one = jnp.ones_like(x)
        pick = lambda first, *values: functools.reduce(
            lambda rest, kv: jnp.where(term == kv[0], kv[1], rest),
            enumerate(values, first), jnp.zeros_like(x),
        )
        moments[:, :LANES] = pick(0, one, x, y, x * x, x * y, y * y).astype(bf16)
        moments[:, LANES : 2 * LANES] = pick(6, one, x, y).astype(bf16)
        moments[:, 2 * LANES :] = pick(9, one).astype(bf16)

    live = LIST - pads_ref[0, tile]
    shift_x, shift_y = offset_ref[0, 0] - 16.5, offset_ref[0, 1] - 16.5
    sub = iota((8, LANES), 0)

    lane = iota((BLOCK, LANES), 1)
    own = (lane % 4) == (iota((BLOCK, LANES), 0) // 32)
    rank = jnp.where(iota((8, LANES), 1) // 4 == iota((8, LANES), 0), 1.0, 0.0).astype(bf16)
    spread = []
    for k in range(LIST):
        at = pl.multiple_of((tile * LIST + k) * slices, slices)
        piece = rows[pl.ds(at, slices), 4 * F :]
        piece = jnp.concatenate([piece] * 4, axis=0).astype(f32)
        spread.append(jnp.where(own, piece, 0.0).astype(bf16))
        feat = jnp.concatenate(
            [rows[pl.ds(at, slices), F * i : F * (i + 1)] for i in range(4)], axis=0
        )
        feats[BLOCK * k : BLOCK * (k + 1), :] = feat
        feats_t[:, BLOCK * k : BLOCK * (k + 1)] = feat.astype(f32).T.astype(bf16)
    table = dot(rank, jnp.concatenate(spread, axis=0), NT)
    cx, cy = table[0:1] + shift_x, table[1:2] + shift_y
    a, c = jnp.exp(table[2:3]), jnp.exp(table[3:4])
    root = jnp.exp(0.5 * (table[2:3] + table[3:4]))
    b, logit = table[4:5] * root, table[5:6]

    h = -0.5 * LOG2E
    level = -LOG2E * jnp.log(1.0 + jnp.exp(-logit))
    level = level + h * (a * cx * cx + 2.0 * b * cx * cy + c * cy * cy)
    terms = jnp.concatenate(
        [
            jnp.where(iota((1, EVERY), 1) // BLOCK < live, level, -1e30),
            (-2.0 * h) * (a * cx + b * cy),
            (-2.0 * h) * (b * cx + c * cy),
            h * a,
            (2.0 * h) * b,
            h * c,
            jnp.zeros((2, EVERY), f32),
        ],
        axis=0,
    )
    high = terms.astype(bf16).astype(f32)
    middle = (terms - high).astype(bf16).astype(f32)
    parts = [high, middle, terms - high - middle]
    for k in range(LIST):
        square = [part[:, BLOCK * k : BLOCK * (k + 1)] for part in parts]
        square = jnp.concatenate(square + [jnp.zeros((LANES - 24, LANES), f32)], axis=0)
        coefs[BLOCK * k : BLOCK * (k + 1), :] = square.T.astype(bf16)

    trans[...] = jnp.ones_like(trans)
    below[...] = jnp.zeros_like(below)

    def forward(k):
        first = pl.multiple_of(k * BLOCK, BLOCK)
        coef = coefs[pl.ds(first, BLOCK), :]
        for chunk in range(CHUNKS):
            columns = slice(chunk * LANES, (chunk + 1) * LANES)
            alpha = jnp.exp2(dot(coef, basis[:, columns]))
            keep = 1.0 - alpha
            ratios[pl.ds(first, BLOCK), columns] = alpha / keep
            before, run = [None] * 16, None
            for v in VISIT:
                before[v] = run
                piece = keep[8 * v : 8 * v + 8]
                run = piece if run is None else run * piece
            for step in (1, 2, 4):
                run = run * jnp.where(sub >= step, pltpu.roll(run, step, 0), 1.0)
            carry = trans[8 * chunk : 8 * chunk + 8]
            start = carry * jnp.where(sub >= 1, pltpu.roll(run, 1, 0), 1.0)
            trans[8 * chunk : 8 * chunk + 8] = carry * jnp.broadcast_to(run[7:8], (8, LANES))
            out = []
            for v in range(16):
                reach = start if before[v] is None else start * before[v]
                out.append(alpha[8 * v : 8 * v + 8] * reach)
            weight = jnp.concatenate(out, axis=0)
            weights[pl.ds(first, BLOCK), columns] = weight
            weights_b[pl.ds(first, BLOCK), columns] = weight.astype(bf16)

    def backward(k):
        first = pl.multiple_of(k * BLOCK, BLOCK)
        feat = feats[pl.ds(first, BLOCK), :]
        for chunk in range(CHUNKS):
            columns = slice(chunk * LANES, (chunk + 1) * LANES)
            slope = dot(feat, grad_ref[0, 0, columns, :], NT)
            gain = slope * weights[pl.ds(first, BLOCK), columns]
            after, run = [None] * 16, None
            for v in VISIT[::-1]:
                after[v] = run
                piece = gain[8 * v : 8 * v + 8]
                run = piece if run is None else run + piece
            for shift in (1, 2, 4):
                run = run + jnp.where(sub < 8 - shift, pltpu.roll(run, 8 - shift, 0), 0.0)
            carry = below[8 * chunk : 8 * chunk + 8]
            start = carry + jnp.where(sub < 7, pltpu.roll(run, 7, 0), 0.0)
            below[8 * chunk : 8 * chunk + 8] = carry + jnp.broadcast_to(run[0:1], (8, LANES))
            out = []
            for v in range(16):
                rest = start if after[v] is None else start + after[v]
                ratio = ratios[pl.ds(first + 8 * v, 8), columns]
                out.append(gain[8 * v : 8 * v + 8] - rest * ratio)
            deltas[:, columns] = jnp.concatenate(out, axis=0)
        for v in range(16):
            once = twice = thrice = None
            for chunk in range(CHUNKS):
                piece = deltas[8 * v : 8 * v + 8, chunk * LANES : (chunk + 1) * LANES]
                once = piece if once is None else once + piece
                twice = once if twice is None else twice + once
                thrice = twice if thrice is None else thrice + twice
            at = pl.ds(first + 8 * v, 8)
            sums[at, :LANES] = once
            sums[at, LANES : 2 * LANES] = twice
            sums[at, 2 * LANES :] = thrice

    def both(step, entry):
        for n in range(UNROLL):
            entry(step * UNROLL + n)

    lax.fori_loop(0, LIST // UNROLL, lambda step, u: (both(step, forward), u)[1], 0)
    image_ref[0, 0] = dot(feats_t[...], weights_b[...]).T.astype(bf16)
    lax.fori_loop(
        0, LIST // UNROLL, lambda step, u: (both(step, lambda n: backward(LIST - 1 - n)), u)[1], 0
    )

    pulled = dot(weights_b[...], grad_ref[0, 0]).astype(bf16)
    high = sums[...].astype(bf16)
    middle = (sums[...] - high.astype(f32)).astype(bf16)
    table = dot(moments[...], high, NT) + dot(moments[...], middle, NT)
    s, sx, sy, sxx, sxy, syy, t, tx, ty, w = (table[n : n + 1] for n in range(10))
    m0, mx, mxx = s, sx, sxx
    my = sy + 16.0 * s - 4.0 * t
    mxy = sxy + 16.0 * sx - 4.0 * tx
    myy = syy + 32.0 * sy + 256.0 * s - 8.0 * ty - 144.0 * t + 32.0 * w
    dx, dy = mx - cx * m0, my - cy * m0
    dxx = mxx - 2.0 * cx * mx + cx * cx * m0
    dxy = mxy - cx * my - cy * mx + cx * cy * m0
    dyy = myy - 2.0 * cy * my + cy * cy * m0
    grads = jnp.concatenate(
        [
            a * dx + b * dy,
            b * dx + c * dy,
            -0.5 * (a * dxx + b * dxy),
            -0.5 * (c * dyy + b * dxy),
            -root * dxy,
            m0 / (1.0 + jnp.exp(logit)),
            jnp.zeros((2, EVERY), f32),
        ],
        axis=0,
    )
    high = grads.astype(bf16).astype(f32)
    low = grads - high
    group = iota((8, LANES), 1) // 32
    for k in range(LIST):
        pair = [part[:, BLOCK * k : BLOCK * (k + 1)] for part in (high, low)]
        pair = [jnp.where(group == i, part, 0.0) for part in pair for i in range(4)]
        pair.append(jnp.zeros((LANES - 64, LANES), f32))
        turned = jnp.concatenate(pair, axis=0).T
        packed = turned[0:32] + turned[32:64] + turned[64:96] + turned[96:128]
        at = pl.multiple_of((tile * LIST + k) * slices, slices)
        for i in range(4):
            first = BLOCK * k + 32 * i
            back[pl.ds(at, slices), F * i : F * (i + 1)] = pulled[first : first + 32]
        back[pl.ds(at, slices), 4 * F :] = packed.astype(bf16)

    @pl.when(tile == 1)
    def _():
        sent_ref[...] = dot(perm[...], back[...], TN).astype(bf16)


def finish_kernel(slab_ref, centers_ref, scales_ref, corr_ref, opac_ref, feats_ref, wide, tall):
    slices, held = slab_ref.shape[0], slab_ref.shape[1]
    for n in range(slices):
        for i in range(5):
            wide[i, held * n : held * (n + 1), :] = slab_ref[n, :, F * i : F * (i + 1)].astype(f32)
    lane = iota((slices, LANES), 1)
    place = jnp.where(lane < 64, (lane % 32) // 8, -1)
    for n in range(held):
        at = pl.ds(n, slices, stride=held)
        small = wide[4, at, :]
        for i in range(4):
            feats_ref[n, pl.ds(i, slices, stride=4), :] = wide[i, at, :]
            tall[pl.ds(BLOCK * n + i, slices, stride=4), :] = jnp.where(place == i, small, 0.0)
    rank = jnp.where(iota((8, LANES), 1) % 8 == iota((8, LANES), 0), 1.0, 0.0).astype(bf16)
    table = dot(rank, tall[...].astype(bf16), NT)
    for n in range(held):
        own = table[:, BLOCK * n : BLOCK * (n + 1)]
        centers_ref[n] = own[0:2]
        scales_ref[n] = own[2:4]
        corr_ref[n : n + 1, :] = own[4:5]
        opac_ref[n : n + 1, :] = own[5:6]


def cut_kernel(view_ref, centers_ref, scales_ref, corr_ref, opac_ref, feats_ref, out_ref, pairs):
    held = feats_ref.shape[0]
    view = view_ref[0]
    part = 4
    base = pl.multiple_of((view // 4) * 16, 16)
    near = feats_ref[:, pl.ds(base, 16), :].reshape(held * 16, F)
    row, column = iota((held, held * 16), 0), iota((held, held * 16), 1)
    cuts = []
    for i in range(part):
        hot = jnp.where(column == row * 16 + (view % 4) * part + i, 1.0, 0.0).astype(bf16)
        cuts.append(dot(hot, near))
    for n in range(held):
        pairs[0, 2 * n : 2 * n + 2, :] = centers_ref[n].astype(f32)
        pairs[1, 2 * n : 2 * n + 2, :] = scales_ref[n].astype(f32)
    row, column = iota((held, 2 * held), 0), iota((held, 2 * held), 1)
    params = []
    for which in range(2):
        for j in range(2):
            hot = jnp.where(column == 2 * row + j, 1.0, 0.0).astype(bf16)
            params.append(dot(hot, pairs[which].astype(bf16)).astype(bf16))
    params += [corr_ref[...], opac_ref[...]]
    gauss, lane = iota((BLOCK, LANES), 0) - view * part, iota((BLOCK, LANES), 1)
    small = jnp.zeros((held, LANES), f32)
    for j, param in enumerate(params):
        chosen = (lane == gauss + part * j) & (gauss >= 0) & (gauss < part)
        small = small + dot(param, jnp.where(chosen, 1.0, 0.0).astype(bf16))
    slab = jnp.concatenate(cuts + [small], axis=1).astype(bf16)
    for n in range(out_ref.shape[0]):
        out_ref[n] = slab


def in_vmem(kernel, shape, *args):
    spec = pl.BlockSpec(memory_space=pltpu.VMEM)
    args = [pltpu.with_memory_space_constraint(arg, pltpu.VMEM) for arg in args]
    return pl.pallas_call(
        kernel, out_shape=pltpu.VMEM(shape, bf16), in_specs=[spec] * len(args), out_specs=spec
    )(*args)


def tile_call(pads, offset, blocks, grad):
    count = blocks.shape[0]
    smem = pl.BlockSpec(memory_space=pltpu.SMEM)
    whole = pl.BlockSpec((count, WIDTH), lambda t: (0, 0))
    image = pl.BlockSpec((1, 1, PIX, F), lambda t: (0, t, 0, 0))
    return pl.pallas_call(
        tile_kernel,
        grid=(2,),
        out_shape=(
            jax.ShapeDtypeStruct(grad.shape, bf16),
            jax.ShapeDtypeStruct((count, WIDTH), bf16),
        ),
        in_specs=[smem, smem, whole, image],
        out_specs=(image, whole),
        scratch_shapes=[
            pltpu.VMEM((count, WIDTH), bf16),
            pltpu.VMEM((count, count), bf16),
            pltpu.VMEM((LANES, PIX), bf16),
            pltpu.VMEM((16, 3 * LANES), bf16),
            pltpu.VMEM((EVERY, F), bf16),
            pltpu.VMEM((F, EVERY), bf16),
            pltpu.VMEM((EVERY, LANES), bf16),
            pltpu.VMEM((EVERY, PIX), f32),
            pltpu.VMEM((EVERY, PIX), bf16),
            pltpu.VMEM((EVERY, PIX), f32),
            pltpu.VMEM((BLOCK, PIX), f32),
            pltpu.VMEM((EVERY, 3 * LANES), f32),
            pltpu.VMEM((8 * CHUNKS, LANES), f32),
            pltpu.VMEM((8 * CHUNKS, LANES), f32),
            pltpu.VMEM((count, WIDTH), bf16),
        ],
        compiler_params=pltpu.CompilerParams(vmem_limit_bytes=48 * 1024 * 1024),
    )(pads, offset, blocks, grad)


def shards(
    centers,
    log_scales,
    correlation,
    opacity_logit,
    features,
    view_offset,
    block_list,
    pad_count,
    block_home,
    image_grad,
):
    views, tiles = lax.axis_size("view"), lax.axis_size("tile")
    held = centers.shape[0]
    total = held * tiles
    view = lax.axis_index("view")

    def exchange(x, axis):
        return lax.all_to_all(x, axis, split_axis=0, concat_axis=0, tiled=True)

    spec = pl.BlockSpec(memory_space=pltpu.VMEM)
    slab = pl.pallas_call(
        cut_kernel,
        out_shape=pltpu.VMEM((tiles, held, WIDTH), bf16),
        in_specs=[pl.BlockSpec(memory_space=pltpu.SMEM)] + [spec] * 5,
        out_specs=spec,
        scratch_shapes=[pltpu.VMEM((2, 2 * held, LANES), f32)],
    )(view.reshape(1), centers, log_scales, correlation, opacity_logit, features)
    table = exchange(slab, "tile")
    rows = jnp.take(block_home, block_list.reshape(-1))
    slots = rows.shape[0]
    asked = lax.all_gather(rows, "view")
    table, ids = table.reshape(total, WIDTH), asked.reshape(1, -1)
    wanted = in_vmem(gather_kernel, (views * slots, WIDTH), ids, table)
    blocks = exchange(wanted, "view")

    image, sent = tile_call(pad_count, view_offset, blocks, image_grad)

    came = exchange(sent, "view")
    partial = in_vmem(scatter_kernel, (total, WIDTH), ids, came)
    partial = exchange(partial, "tile").reshape(tiles, held, WIDTH)
    slab = in_vmem(sum_kernel, (views, held, WIDTH), partial)
    slab = exchange(slab, "view")

    shape = lambda *dims: jax.ShapeDtypeStruct(dims, f32)
    spec = pl.BlockSpec(memory_space=pltpu.VMEM)
    grads = pl.pallas_call(
        finish_kernel,
        out_shape=(
            shape(held, 2, BLOCK), shape(held, 2, BLOCK), shape(held, BLOCK), shape(held, BLOCK),
            shape(held, BLOCK, F),
        ),
        in_specs=[spec],
        out_specs=(spec,) * 5,
        scratch_shapes=[
            pltpu.VMEM((5, views * held, LANES), f32),
            pltpu.VMEM((held * BLOCK, LANES), f32),
        ],
    )(pltpu.with_memory_space_constraint(slab, pltpu.VMEM))
    return (image, *grads)


def solution(mesh):
    in_specs = (
        P("tile", None, None),
        P("tile", None, None),
        P("tile", None),
        P("tile", None),
        P("tile", None, None),
        P("view", None),
        P("view", "tile", None),
        P("view", "tile"),
        P(),
        P("view", "tile", None, None),
    )
    out_specs = (
        P("view", "tile", None, None),
        P("tile", None, None),
        P("tile", None, None),
        P("tile", None),
        P("tile", None),
        P("tile", None, None),
    )
    return jax.shard_map(shards, mesh=mesh, in_specs=in_specs, out_specs=out_specs, check_vma=False)
```

```python
import functools

import jax
import jax.numpy as jnp
from jax import lax
from jax.experimental import pallas as pl
from jax.experimental.pallas import tpu as pltpu
from jax.sharding import PartitionSpec as P


TILE_W = 32
PIX = 1024
F = 128
BLOCK = 128
LIST = 8
LANES = 128
WIDTH = 640
HELD = 24
SENT = 4 * HELD + 8
LOG2E = 1.4426950408889634
CHUNKS = PIX // LANES
UNROLL = 8
f32 = jnp.float32
bf16 = jnp.bfloat16

NN = (((1,), (0,)), ((), ()))
NT = (((1,), (1,)), ((), ()))
TN = (((0,), (0,)), ((), ()))


def dot(a, b, dims=NN, precision=None):
    return lax.dot_general(a, b, dims, precision=precision, preferred_element_type=f32)


def iota(shape, dim):
    return lax.broadcasted_iota(jnp.int32, shape, dim)


def lane_roll(x, shift):
    return pltpu.roll(x, shift % LANES, 1)


def fold_pairs(x):
    return x + lane_roll(x, -32)


def one_hot(mask):
    return jnp.where(mask, 1.0, 0.0).astype(bf16)


def pack_rows(x):
    shards_here = x.shape[0] // HELD
    row, column = iota((8 * shards_here, x.shape[0]), 0), iota((8 * shards_here, x.shape[0]), 1)
    out = jnp.zeros((8 * shards_here, LANES), f32)
    for q in range(4):
        hot = one_hot((column == (row // 8) * HELD + 6 * q + row % 8) & (row % 8 < 6))
        out = out + lane_roll(dot(hot, x), 32 * q)
    return out


def unpack_rows(x):
    shards_here = x.shape[0] // 8
    row, column = iota((HELD * shards_here, x.shape[0]), 0), iota((HELD * shards_here, x.shape[0]), 1)
    out = jnp.zeros((HELD * shards_here, LANES), f32)
    for q in range(4):
        hot = one_hot((row == (column // 8) * HELD + 6 * q + column % 8) & (column % 8 < 6))
        piece = jnp.where(iota(x.shape, 1) < 32, lane_roll(x, -32 * q), 0.0)
        out = out + dot(hot, piece.astype(bf16))
    return out


def gather_kernel(ids_ref, table_ref, out_ref, wide):
    tiles = table_ref.shape[0]
    rows, count = tiles * HELD, ids_ref.shape[1]
    for z in range(tiles):
        for i in range(4):
            wide[HELD * z : HELD * (z + 1), F * i : F * (i + 1)] = table_ref[
                z, HELD * i : HELD * (i + 1), :
            ].astype(f32)
    small = [table_ref[z, 4 * HELD :, :].astype(f32) for z in range(tiles)]
    wide[:, 4 * F :] = unpack_rows(jnp.concatenate(small, axis=0))
    hot = one_hot(iota((rows, count), 0) == ids_ref[...])
    out_ref[...] = dot(hot, wide[...].astype(bf16), TN).astype(bf16)


def scatter_kernel(ids_ref, grads_ref, out_ref):
    tiles = out_ref.shape[0]
    rows, count = tiles * HELD, ids_ref.shape[1]
    hot = one_hot(iota((rows, count), 0) == ids_ref[...])
    total = dot(hot, grads_ref[...])
    small = fold_pairs(total[:, 4 * F :])
    small = pack_rows(jnp.where(iota(small.shape, 1) < 32, small, 0.0).astype(bf16))
    for z in range(tiles):
        for i in range(4):
            out_ref[z, HELD * i : HELD * (i + 1), :] = total[
                HELD * z : HELD * (z + 1), F * i : F * (i + 1)
            ].astype(bf16)
        out_ref[z, 4 * HELD :, :] = small[8 * z : 8 * z + 8].astype(bf16)


def sum_kernel(parts_ref, out_ref):
    total = parts_ref[0].astype(f32)
    for n in range(1, parts_ref.shape[0]):
        total = total + parts_ref[n].astype(f32)
    small = total[4 * HELD :]
    high = small.astype(bf16).astype(f32)
    pairs = unpack_rows(high) + lane_roll(unpack_rows(small - high), 32)
    parts = [total[HELD * i : HELD * (i + 1)] for i in range(4)] + [pairs]
    total = jnp.concatenate(parts, axis=1).astype(bf16)
    for n in range(out_ref.shape[0]):
        out_ref[n] = total


def slot_permutation(slices, slots):
    count = slices * slots
    row, column = iota((count, count), 0), iota((count, count), 1)
    slot, place = row // slices, row % slices
    piece = (place % 8) * 4 + place // 8
    return jnp.where(column == piece * slots + slot, 1.0, 0.0).astype(bf16)


VISIT = [(t % 4) * 4 + t // 4 for t in range(16)]
EVERY = LIST * BLOCK


def tile_kernel(
    pads_ref, offset_ref, blocks_ref, grad_ref, image_ref, sent_ref,
    rows, perm, basis, moments, feats, feats_t, coefs, weights, weights_b, ratios, deltas, sums, trans, below, back,
):
    tile = pl.program_id(0)
    slots = 2 * LIST
    slices = 32

    @pl.when(tile == 0)
    def _():
        perm[...] = slot_permutation(slices, slots)
        rows[...] = dot(perm[...], blocks_ref[...]).astype(bf16)
        term, pixel = iota((LANES, PIX), 0), iota((LANES, PIX), 1)
        across, down = (pixel % TILE_W - 16).astype(f32), (pixel // TILE_W - 16).astype(f32)
        kind = jnp.where(term < 24, term % 8, 7)
        value = jnp.where(
            kind == 0, 1.0,
            jnp.where(kind == 1, across,
            jnp.where(kind == 2, down,
            jnp.where(kind == 3, across * across,
            jnp.where(kind == 4, across * down,
            jnp.where(kind == 5, down * down, 0.0))))))
        basis[...] = value.astype(bf16)
        term, lane = iota((16, LANES), 0), iota((16, LANES), 1)
        x, y = (lane % TILE_W - 16).astype(f32), (lane // TILE_W).astype(f32)
        one = jnp.ones_like(x)
        pick = lambda first, *values: functools.reduce(
            lambda rest, kv: jnp.where(term == kv[0], kv[1], rest),
            enumerate(values, first), jnp.zeros_like(x),
        )
        moments[:, :LANES] = pick(0, one, x, y, x * x, x * y, y * y).astype(bf16)
        moments[:, LANES : 2 * LANES] = pick(6, one, x, y).astype(bf16)
        moments[:, 2 * LANES :] = pick(9, one).astype(bf16)

    live = LIST - pads_ref[0, tile]
    shift_x, shift_y = offset_ref[0, 0] - 16.5, offset_ref[0, 1] - 16.5
    sub = iota((8, LANES), 0)

    lane = iota((BLOCK, LANES), 1)
    own = (lane % 4) == (iota((BLOCK, LANES), 0) // 32)
    rank = jnp.where(iota((8, LANES), 1) // 4 == iota((8, LANES), 0), 1.0, 0.0).astype(bf16)
    spread = []
    for k in range(LIST):
        at = pl.multiple_of((tile * LIST + k) * slices, slices)
        piece = rows[pl.ds(at, slices), 4 * F :]
        piece = jnp.concatenate([piece] * 4, axis=0).astype(f32)
        spread.append(jnp.where(own, piece, 0.0).astype(bf16))
        feat = jnp.concatenate(
            [rows[pl.ds(at, slices), F * i : F * (i + 1)] for i in range(4)], axis=0
        )
        feats[BLOCK * k : BLOCK * (k + 1), :] = feat
        feats_t[:, BLOCK * k : BLOCK * (k + 1)] = feat.astype(f32).T.astype(bf16)
    table = dot(rank, jnp.concatenate(spread, axis=0), NT)
    cx, cy = table[0:1] + shift_x, table[1:2] + shift_y
    a, c = jnp.exp(table[2:3]), jnp.exp(table[3:4])
    root = jnp.exp(0.5 * (table[2:3] + table[3:4]))
    b, logit = table[4:5] * root, table[5:6]

    h = -0.5 * LOG2E
    level = -LOG2E * jnp.log(1.0 + jnp.exp(-logit))
    level = level + h * (a * cx * cx + 2.0 * b * cx * cy + c * cy * cy)
    terms = jnp.concatenate(
        [
            jnp.where(iota((1, EVERY), 1) // BLOCK < live, level, -1e30),
            (-2.0 * h) * (a * cx + b * cy),
            (-2.0 * h) * (b * cx + c * cy),
            h * a,
            (2.0 * h) * b,
            h * c,
            jnp.zeros((2, EVERY), f32),
        ],
        axis=0,
    )
    high = terms.astype(bf16).astype(f32)
    middle = (terms - high).astype(bf16).astype(f32)
    parts = [high, middle, terms - high - middle]
    for k in range(LIST):
        square = [part[:, BLOCK * k : BLOCK * (k + 1)] for part in parts]
        square = jnp.concatenate(square + [jnp.zeros((LANES - 24, LANES), f32)], axis=0)
        coefs[BLOCK * k : BLOCK * (k + 1), :] = square.T.astype(bf16)

    trans[...] = jnp.ones_like(trans)
    below[...] = jnp.zeros_like(below)

    def forward(k):
        first = pl.multiple_of(k * BLOCK, BLOCK)
        coef = coefs[pl.ds(first, BLOCK), :]
        for chunk in range(CHUNKS):
            columns = slice(chunk * LANES, (chunk + 1) * LANES)
            alpha = jnp.exp2(dot(coef, basis[:, columns]))
            keep = 1.0 - alpha
            ratios[pl.ds(first, BLOCK), columns] = alpha / keep
            before, run = [None] * 16, None
            for v in VISIT:
                before[v] = run
                piece = keep[8 * v : 8 * v + 8]
                run = piece if run is None else run * piece
            for step in (1, 2, 4):
                run = run * jnp.where(sub >= step, pltpu.roll(run, step, 0), 1.0)
            carry = trans[8 * chunk : 8 * chunk + 8]
            start = carry * jnp.where(sub >= 1, pltpu.roll(run, 1, 0), 1.0)
            trans[8 * chunk : 8 * chunk + 8] = carry * jnp.broadcast_to(run[7:8], (8, LANES))
            out = []
            for v in range(16):
                reach = start if before[v] is None else start * before[v]
                out.append(alpha[8 * v : 8 * v + 8] * reach)
            weight = jnp.concatenate(out, axis=0)
            weights[pl.ds(first, BLOCK), columns] = weight
            weights_b[pl.ds(first, BLOCK), columns] = weight.astype(bf16)

    def backward(k):
        first = pl.multiple_of(k * BLOCK, BLOCK)
        feat = feats[pl.ds(first, BLOCK), :]
        for chunk in range(CHUNKS):
            columns = slice(chunk * LANES, (chunk + 1) * LANES)
            slope = dot(feat, grad_ref[0, 0, columns, :], NT)
            gain = slope * weights[pl.ds(first, BLOCK), columns]
            after, run = [None] * 16, None
            for v in VISIT[::-1]:
                after[v] = run
                piece = gain[8 * v : 8 * v + 8]
                run = piece if run is None else run + piece
            for shift in (1, 2, 4):
                run = run + jnp.where(sub < 8 - shift, pltpu.roll(run, 8 - shift, 0), 0.0)
            carry = below[8 * chunk : 8 * chunk + 8]
            start = carry + jnp.where(sub < 7, pltpu.roll(run, 7, 0), 0.0)
            below[8 * chunk : 8 * chunk + 8] = carry + jnp.broadcast_to(run[0:1], (8, LANES))
            out = []
            for v in range(16):
                rest = start if after[v] is None else start + after[v]
                ratio = ratios[pl.ds(first + 8 * v, 8), columns]
                out.append(gain[8 * v : 8 * v + 8] - rest * ratio)
            deltas[:, columns] = jnp.concatenate(out, axis=0)
        for v in range(16):
            once = twice = thrice = None
            for chunk in range(CHUNKS):
                piece = deltas[8 * v : 8 * v + 8, chunk * LANES : (chunk + 1) * LANES]
                once = piece if once is None else once + piece
                twice = once if twice is None else twice + once
                thrice = twice if thrice is None else thrice + twice
            at = pl.ds(first + 8 * v, 8)
            sums[at, :LANES] = once
            sums[at, LANES : 2 * LANES] = twice
            sums[at, 2 * LANES :] = thrice

    def both(step, entry):
        for n in range(UNROLL):
            entry(step * UNROLL + n)

    lax.fori_loop(0, LIST // UNROLL, lambda step, u: (both(step, forward), u)[1], 0)
    image_ref[0, 0] = dot(feats_t[...], weights_b[...]).T.astype(bf16)
    lax.fori_loop(
        0, LIST // UNROLL, lambda step, u: (both(step, lambda n: backward(LIST - 1 - n)), u)[1], 0
    )

    pulled = dot(weights_b[...], grad_ref[0, 0]).astype(bf16)
    high = sums[...].astype(bf16)
    middle = (sums[...] - high.astype(f32)).astype(bf16)
    table = dot(moments[...], high, NT) + dot(moments[...], middle, NT)
    s, sx, sy, sxx, sxy, syy, t, tx, ty, w = (table[n : n + 1] for n in range(10))
    m0, mx, mxx = s, sx, sxx
    my = sy + 16.0 * s - 4.0 * t
    mxy = sxy + 16.0 * sx - 4.0 * tx
    myy = syy + 32.0 * sy + 256.0 * s - 8.0 * ty - 144.0 * t + 32.0 * w
    dx, dy = mx - cx * m0, my - cy * m0
    dxx = mxx - 2.0 * cx * mx + cx * cx * m0
    dxy = mxy - cx * my - cy * mx + cx * cy * m0
    dyy = myy - 2.0 * cy * my + cy * cy * m0
    grads = jnp.concatenate(
        [
            a * dx + b * dy,
            b * dx + c * dy,
            -0.5 * (a * dxx + b * dxy),
            -0.5 * (c * dyy + b * dxy),
            -root * dxy,
            m0 / (1.0 + jnp.exp(logit)),
            jnp.zeros((2, EVERY), f32),
        ],
        axis=0,
    )
    high = grads.astype(bf16).astype(f32)
    low = grads - high
    group = iota((8, LANES), 1) // 32
    for k in range(LIST):
        pair = [part[:, BLOCK * k : BLOCK * (k + 1)] for part in (high, low)]
        pair = [jnp.where(group == i, part, 0.0) for part in pair for i in range(4)]
        pair.append(jnp.zeros((LANES - 64, LANES), f32))
        turned = jnp.concatenate(pair, axis=0).T
        packed = turned[0:32] + turned[32:64] + turned[64:96] + turned[96:128]
        at = pl.multiple_of((tile * LIST + k) * slices, slices)
        for i in range(4):
            first = BLOCK * k + 32 * i
            back[pl.ds(at, slices), F * i : F * (i + 1)] = pulled[first : first + 32]
        back[pl.ds(at, slices), 4 * F :] = packed.astype(bf16)

    @pl.when(tile == 1)
    def _():
        sent_ref[...] = dot(perm[...], back[...], TN).astype(bf16)


def finish_kernel(slab_ref, centers_ref, scales_ref, corr_ref, opac_ref, feats_ref, wide, tall):
    slices, held = slab_ref.shape[0], slab_ref.shape[1]
    for n in range(slices):
        for i in range(5):
            wide[i, held * n : held * (n + 1), :] = slab_ref[n, :, F * i : F * (i + 1)].astype(f32)
    lane = iota((slices, LANES), 1)
    place = jnp.where(lane < 64, (lane % 32) // 8, -1)
    for n in range(held):
        at = pl.ds(n, slices, stride=held)
        small = wide[4, at, :]
        for i in range(4):
            feats_ref[n, pl.ds(i, slices, stride=4), :] = wide[i, at, :]
            tall[pl.ds(BLOCK * n + i, slices, stride=4), :] = jnp.where(place == i, small, 0.0)
    rank = jnp.where(iota((8, LANES), 1) % 8 == iota((8, LANES), 0), 1.0, 0.0).astype(bf16)
    table = dot(rank, tall[...].astype(bf16), NT)
    for n in range(held):
        own = table[:, BLOCK * n : BLOCK * (n + 1)]
        centers_ref[n] = own[0:2]
        scales_ref[n] = own[2:4]
        corr_ref[n : n + 1, :] = own[4:5]
        opac_ref[n : n + 1, :] = own[5:6]


def cut_kernel(view_ref, centers_ref, scales_ref, corr_ref, opac_ref, feats_ref, out_ref, pairs):
    held = feats_ref.shape[0]
    view = view_ref[0]
    part = 4
    base = pl.multiple_of((view // 4) * 16, 16)
    near = feats_ref[:, pl.ds(base, 16), :].reshape(held * 16, F)
    row, column = iota((held, held * 16), 0), iota((held, held * 16), 1)
    cuts = []
    for i in range(part):
        hot = jnp.where(column == row * 16 + (view % 4) * part + i, 1.0, 0.0).astype(bf16)
        cuts.append(dot(hot, near))
    for n in range(held):
        pairs[0, 2 * n : 2 * n + 2, :] = centers_ref[n].astype(f32)
        pairs[1, 2 * n : 2 * n + 2, :] = scales_ref[n].astype(f32)
    row, column = iota((held, 2 * held), 0), iota((held, 2 * held), 1)
    params = []
    for which in range(2):
        for j in range(2):
            hot = jnp.where(column == 2 * row + j, 1.0, 0.0).astype(bf16)
            params.append(dot(hot, pairs[which].astype(bf16)).astype(bf16))
    params += [corr_ref[...], opac_ref[...]]
    gauss, lane = iota((BLOCK, LANES), 0) - view * part, iota((BLOCK, LANES), 1)
    small = jnp.zeros((held, LANES), f32)
    for j, param in enumerate(params):
        chosen = (lane == gauss + part * j) & (gauss >= 0) & (gauss < part)
        small = small + dot(param, jnp.where(chosen, 1.0, 0.0).astype(bf16))
    slab = jnp.concatenate(cuts + [pack_rows(small.astype(bf16))], axis=0).astype(bf16)
    for n in range(out_ref.shape[0]):
        out_ref[n] = slab


def in_vmem(kernel, shape, *args, scratch=()):
    spec = pl.BlockSpec(memory_space=pltpu.VMEM)
    args = [pltpu.with_memory_space_constraint(arg, pltpu.VMEM) for arg in args]
    return pl.pallas_call(
        kernel,
        out_shape=pltpu.VMEM(shape, bf16),
        in_specs=[spec] * len(args),
        out_specs=spec,
        scratch_shapes=scratch,
    )(*args)


def tile_call(pads, offset, blocks, grad):
    count = blocks.shape[0]
    smem = pl.BlockSpec(memory_space=pltpu.SMEM)
    whole = pl.BlockSpec((count, WIDTH), lambda t: (0, 0))
    image = pl.BlockSpec((1, 1, PIX, F), lambda t: (0, t, 0, 0))
    return pl.pallas_call(
        tile_kernel,
        grid=(2,),
        out_shape=(
            jax.ShapeDtypeStruct(grad.shape, bf16),
            jax.ShapeDtypeStruct((count, WIDTH), bf16),
        ),
        in_specs=[smem, smem, whole, image],
        out_specs=(image, whole),
        scratch_shapes=[
            pltpu.VMEM((count, WIDTH), bf16),
            pltpu.VMEM((count, count), bf16),
            pltpu.VMEM((LANES, PIX), bf16),
            pltpu.VMEM((16, 3 * LANES), bf16),
            pltpu.VMEM((EVERY, F), bf16),
            pltpu.VMEM((F, EVERY), bf16),
            pltpu.VMEM((EVERY, LANES), bf16),
            pltpu.VMEM((EVERY, PIX), f32),
            pltpu.VMEM((EVERY, PIX), bf16),
            pltpu.VMEM((EVERY, PIX), f32),
            pltpu.VMEM((BLOCK, PIX), f32),
            pltpu.VMEM((EVERY, 3 * LANES), f32),
            pltpu.VMEM((8 * CHUNKS, LANES), f32),
            pltpu.VMEM((8 * CHUNKS, LANES), f32),
            pltpu.VMEM((count, WIDTH), bf16),
        ],
        compiler_params=pltpu.CompilerParams(vmem_limit_bytes=48 * 1024 * 1024),
    )(pads, offset, blocks, grad)


def shards(
    centers,
    log_scales,
    correlation,
    opacity_logit,
    features,
    view_offset,
    block_list,
    pad_count,
    block_home,
    image_grad,
):
    views, tiles = lax.axis_size("view"), lax.axis_size("tile")
    held = centers.shape[0]
    total = held * tiles
    view = lax.axis_index("view")

    def exchange(x, axis):
        return lax.all_to_all(x, axis, split_axis=0, concat_axis=0, tiled=True)

    spec = pl.BlockSpec(memory_space=pltpu.VMEM)
    slab = pl.pallas_call(
        cut_kernel,
        out_shape=pltpu.VMEM((tiles, SENT, LANES), bf16),
        in_specs=[pl.BlockSpec(memory_space=pltpu.SMEM)] + [spec] * 5,
        out_specs=spec,
        scratch_shapes=[pltpu.VMEM((2, 2 * held, LANES), f32)],
    )(view.reshape(1), centers, log_scales, correlation, opacity_logit, features)
    table = exchange(slab, "tile")
    rows = jnp.take(block_home, block_list.reshape(-1))
    slots = rows.shape[0]
    asked = lax.all_gather(rows, "view")
    ids = asked.reshape(1, -1)
    wanted = in_vmem(
        gather_kernel, (views * slots, WIDTH), ids, table,
        scratch=[pltpu.VMEM((total, WIDTH), f32)],
    )
    blocks = exchange(wanted, "view")

    image, sent = tile_call(pad_count, view_offset, blocks, image_grad)

    came = exchange(sent, "view")
    partial = in_vmem(scatter_kernel, (tiles, SENT, LANES), ids, came)
    partial = exchange(partial, "tile")
    slab = in_vmem(sum_kernel, (views, held, WIDTH), partial)
    slab = exchange(slab, "view")

    shape = lambda *dims: jax.ShapeDtypeStruct(dims, f32)
    spec = pl.BlockSpec(memory_space=pltpu.VMEM)
    grads = pl.pallas_call(
        finish_kernel,
        out_shape=(
            shape(held, 2, BLOCK), shape(held, 2, BLOCK), shape(held, BLOCK), shape(held, BLOCK),
            shape(held, BLOCK, F),
        ),
        in_specs=[spec],
        out_specs=(spec,) * 5,
        scratch_shapes=[
            pltpu.VMEM((5, views * held, LANES), f32),
            pltpu.VMEM((held * BLOCK, LANES), f32),
        ],
    )(pltpu.with_memory_space_constraint(slab, pltpu.VMEM))
    return (image, *grads)


def solution(mesh):
    in_specs = (
        P("tile", None, None),
        P("tile", None, None),
        P("tile", None),
        P("tile", None),
        P("tile", None, None),
        P("view", None),
        P("view", "tile", None),
        P("view", "tile"),
        P(),
        P("view", "tile", None, None),
    )
    out_specs = (
        P("view", "tile", None, None),
        P("tile", None, None),
        P("tile", None, None),
        P("tile", None),
        P("tile", None),
        P("tile", None, None),
    )
    return jax.shard_map(shards, mesh=mesh, in_specs=in_specs, out_specs=out_specs, check_vma=False)
```

```python
import functools

import jax
import jax.numpy as jnp
from jax import lax
from jax.experimental import pallas as pl
from jax.experimental.pallas import tpu as pltpu
from jax.sharding import PartitionSpec as P


TILE_W = 32
PIX = 1024
F = 128
BLOCK = 128
LIST = 8
LANES = 128
WIDTH = 640
HELD = 24
SENT = 4 * HELD + 8
LOG2E = 1.4426950408889634
CHUNKS = PIX // LANES
UNROLL = 8
f32 = jnp.float32
bf16 = jnp.bfloat16

NN = (((1,), (0,)), ((), ()))
NT = (((1,), (1,)), ((), ()))
TN = (((0,), (0,)), ((), ()))


def dot(a, b, dims=NN, precision=None):
    return lax.dot_general(a, b, dims, precision=precision, preferred_element_type=f32)


def iota(shape, dim):
    return lax.broadcasted_iota(jnp.int32, shape, dim)


def lane_roll(x, shift):
    return pltpu.roll(x, shift % LANES, 1)


def fold_pairs(x):
    return x + lane_roll(x, -32)


def one_hot(mask):
    return jnp.where(mask, 1.0, 0.0).astype(bf16)


def pack_rows(x):
    shards_here = x.shape[0] // HELD
    row, column = iota((8 * shards_here, x.shape[0]), 0), iota((8 * shards_here, x.shape[0]), 1)
    out = jnp.zeros((8 * shards_here, LANES), f32)
    for q in range(4):
        hot = one_hot((column == (row // 8) * HELD + 6 * q + row % 8) & (row % 8 < 6))
        out = out + lane_roll(dot(hot, x), 32 * q)
    return out


def unpack_rows(x):
    shards_here = x.shape[0] // 8
    row, column = iota((HELD * shards_here, x.shape[0]), 0), iota((HELD * shards_here, x.shape[0]), 1)
    out = jnp.zeros((HELD * shards_here, LANES), f32)
    for q in range(4):
        hot = one_hot((row == (column // 8) * HELD + 6 * q + column % 8) & (column % 8 < 6))
        piece = jnp.where(iota(x.shape, 1) < 32, lane_roll(x, -32 * q), 0.0)
        out = out + dot(hot, piece.astype(bf16))
    return out


def gather_kernel(lists_ref, table_ref, out_ref, ids_ref, lists, wide):
    tiles = table_ref.shape[0]
    views, slots = lists.shape
    rows, count = tiles * HELD, views * slots
    for v in range(views):
        lists[v : v + 1, :] = lists_ref[v]
    ids = lists[...]
    hot = one_hot(iota((slots, count), 1) % slots == iota((slots, count), 0))
    ids = 16.0 * dot((ids // 16).astype(f32).astype(bf16), hot) + dot(
        (ids % 16).astype(f32).astype(bf16), hot
    )
    ids = jnp.where(iota((views, count), 1) // slots == iota((views, count), 0), ids, 0.0)
    ids_ref[...] = jnp.sum(ids, axis=0, keepdims=True).astype(jnp.int32)
    for z in range(tiles):
        for i in range(4):
            wide[HELD * z : HELD * (z + 1), F * i : F * (i + 1)] = table_ref[
                z, HELD * i : HELD * (i + 1), :
            ].astype(f32)
    small = [table_ref[z, 4 * HELD :, :].astype(f32) for z in range(tiles)]
    wide[:, 4 * F :] = unpack_rows(jnp.concatenate(small, axis=0))
    hot = one_hot(iota((rows, count), 0) == ids_ref[...])
    out_ref[...] = dot(hot, wide[...].astype(bf16), TN).astype(bf16)


def scatter_kernel(ids_ref, grads_ref, out_ref):
    tiles = out_ref.shape[0]
    rows, count = tiles * HELD, ids_ref.shape[1]
    hot = one_hot(iota((rows, count), 0) == ids_ref[...])
    total = dot(hot, grads_ref[...])
    small = fold_pairs(total[:, 4 * F :])
    small = pack_rows(jnp.where(iota(small.shape, 1) < 32, small, 0.0).astype(bf16))
    for z in range(tiles):
        for i in range(4):
            out_ref[z, HELD * i : HELD * (i + 1), :] = total[
                HELD * z : HELD * (z + 1), F * i : F * (i + 1)
            ].astype(bf16)
        out_ref[z, 4 * HELD :, :] = small[8 * z : 8 * z + 8].astype(bf16)


def sum_kernel(parts_ref, out_ref):
    total = parts_ref[0].astype(f32)
    for n in range(1, parts_ref.shape[0]):
        total = total + parts_ref[n].astype(f32)
    total = total.astype(bf16)
    for n in range(out_ref.shape[0]):
        out_ref[n] = total


def slot_permutation(slices, slots):
    count = slices * slots
    row, column = iota((count, count), 0), iota((count, count), 1)
    slot, place = row // slices, row % slices
    piece = (place % 8) * 4 + place // 8
    return jnp.where(column == piece * slots + slot, 1.0, 0.0).astype(bf16)


VISIT = [(t % 4) * 4 + t // 4 for t in range(16)]
EVERY = LIST * BLOCK


def tile_kernel(
    pads_ref, offset_ref, blocks_ref, grad_ref, image_ref, sent_ref,
    rows, perm, basis, moments, feats, feats_t, coefs, weights, weights_b, ratios, deltas, sums, trans, below, back,
):
    tile = pl.program_id(0)
    slots = 2 * LIST
    slices = 32

    @pl.when(tile == 0)
    def _():
        perm[...] = slot_permutation(slices, slots)
        rows[...] = dot(perm[...], blocks_ref[...]).astype(bf16)
        term, pixel = iota((LANES, PIX), 0), iota((LANES, PIX), 1)
        across, down = (pixel % TILE_W - 16).astype(f32), (pixel // TILE_W - 16).astype(f32)
        kind = jnp.where(term < 24, term % 8, 7)
        value = jnp.where(
            kind == 0, 1.0,
            jnp.where(kind == 1, across,
            jnp.where(kind == 2, down,
            jnp.where(kind == 3, across * across,
            jnp.where(kind == 4, across * down,
            jnp.where(kind == 5, down * down, 0.0))))))
        basis[...] = value.astype(bf16)
        term, lane = iota((16, LANES), 0), iota((16, LANES), 1)
        x, y = (lane % TILE_W - 16).astype(f32), (lane // TILE_W).astype(f32)
        one = jnp.ones_like(x)
        pick = lambda first, *values: functools.reduce(
            lambda rest, kv: jnp.where(term == kv[0], kv[1], rest),
            enumerate(values, first), jnp.zeros_like(x),
        )
        moments[:, :LANES] = pick(0, one, x, y, x * x, x * y, y * y).astype(bf16)
        moments[:, LANES : 2 * LANES] = pick(6, one, x, y).astype(bf16)
        moments[:, 2 * LANES :] = pick(9, one).astype(bf16)

    live = LIST - pads_ref[0, tile]
    shift_x, shift_y = offset_ref[0, 0] - 16.5, offset_ref[0, 1] - 16.5
    sub = iota((8, LANES), 0)

    lane = iota((BLOCK, LANES), 1)
    own = (lane % 4) == (iota((BLOCK, LANES), 0) // 32)
    rank = jnp.where(iota((8, LANES), 1) // 4 == iota((8, LANES), 0), 1.0, 0.0).astype(bf16)
    spread = []
    for k in range(LIST):
        at = pl.multiple_of((tile * LIST + k) * slices, slices)
        piece = rows[pl.ds(at, slices), 4 * F :]
        piece = jnp.concatenate([piece] * 4, axis=0).astype(f32)
        spread.append(jnp.where(own, piece, 0.0).astype(bf16))
        feat = jnp.concatenate(
            [rows[pl.ds(at, slices), F * i : F * (i + 1)] for i in range(4)], axis=0
        )
        feats[BLOCK * k : BLOCK * (k + 1), :] = feat
        feats_t[:, BLOCK * k : BLOCK * (k + 1)] = feat.astype(f32).T.astype(bf16)
    table = dot(rank, jnp.concatenate(spread, axis=0), NT)
    cx, cy = table[0:1] + shift_x, table[1:2] + shift_y
    a, c = jnp.exp(table[2:3]), jnp.exp(table[3:4])
    root = jnp.exp(0.5 * (table[2:3] + table[3:4]))
    b, logit = table[4:5] * root, table[5:6]

    h = -0.5 * LOG2E
    level = -LOG2E * jnp.log(1.0 + jnp.exp(-logit))
    level = level + h * (a * cx * cx + 2.0 * b * cx * cy + c * cy * cy)
    terms = jnp.concatenate(
        [
            jnp.where(iota((1, EVERY), 1) // BLOCK < live, level, -1e30),
            (-2.0 * h) * (a * cx + b * cy),
            (-2.0 * h) * (b * cx + c * cy),
            h * a,
            (2.0 * h) * b,
            h * c,
            jnp.zeros((2, EVERY), f32),
        ],
        axis=0,
    )
    high = terms.astype(bf16).astype(f32)
    middle = (terms - high).astype(bf16).astype(f32)
    parts = [high, middle, terms - high - middle]
    for k in range(LIST):
        square = [part[:, BLOCK * k : BLOCK * (k + 1)] for part in parts]
        square = jnp.concatenate(square + [jnp.zeros((LANES - 24, LANES), f32)], axis=0)
        coefs[BLOCK * k : BLOCK * (k + 1), :] = square.T.astype(bf16)

    trans[...] = jnp.ones_like(trans)
    below[...] = jnp.zeros_like(below)

    def forward(k):
        first = pl.multiple_of(k * BLOCK, BLOCK)
        coef = coefs[pl.ds(first, BLOCK), :]
        for chunk in range(CHUNKS):
            columns = slice(chunk * LANES, (chunk + 1) * LANES)
            alpha = jnp.exp2(dot(coef, basis[:, columns]))
            keep = 1.0 - alpha
            ratios[pl.ds(first, BLOCK), columns] = alpha / keep
            before, run = [None] * 16, None
            for v in VISIT:
                before[v] = run
                piece = keep[8 * v : 8 * v + 8]
                run = piece if run is None else run * piece
            for step in (1, 2, 4):
                run = run * jnp.where(sub >= step, pltpu.roll(run, step, 0), 1.0)
            carry = trans[8 * chunk : 8 * chunk + 8]
            start = carry * jnp.where(sub >= 1, pltpu.roll(run, 1, 0), 1.0)
            trans[8 * chunk : 8 * chunk + 8] = carry * jnp.broadcast_to(run[7:8], (8, LANES))
            out = []
            for v in range(16):
                reach = start if before[v] is None else start * before[v]
                out.append(alpha[8 * v : 8 * v + 8] * reach)
            weight = jnp.concatenate(out, axis=0)
            weights[pl.ds(first, BLOCK), columns] = weight
            weights_b[pl.ds(first, BLOCK), columns] = weight.astype(bf16)

    def backward(k):
        first = pl.multiple_of(k * BLOCK, BLOCK)
        feat = feats[pl.ds(first, BLOCK), :]
        for chunk in range(CHUNKS):
            columns = slice(chunk * LANES, (chunk + 1) * LANES)
            slope = dot(feat, grad_ref[0, 0, columns, :], NT)
            gain = slope * weights[pl.ds(first, BLOCK), columns]
            after, run = [None] * 16, None
            for v in VISIT[::-1]:
                after[v] = run
                piece = gain[8 * v : 8 * v + 8]
                run = piece if run is None else run + piece
            for shift in (1, 2, 4):
                run = run + jnp.where(sub < 8 - shift, pltpu.roll(run, 8 - shift, 0), 0.0)
            carry = below[8 * chunk : 8 * chunk + 8]
            start = carry + jnp.where(sub < 7, pltpu.roll(run, 7, 0), 0.0)
            below[8 * chunk : 8 * chunk + 8] = carry + jnp.broadcast_to(run[0:1], (8, LANES))
            out = []
            for v in range(16):
                rest = start if after[v] is None else start + after[v]
                ratio = ratios[pl.ds(first + 8 * v, 8), columns]
                out.append(gain[8 * v : 8 * v + 8] - rest * ratio)
            deltas[:, columns] = jnp.concatenate(out, axis=0)
        for v in range(16):
            once = twice = thrice = None
            for chunk in range(CHUNKS):
                piece = deltas[8 * v : 8 * v + 8, chunk * LANES : (chunk + 1) * LANES]
                once = piece if once is None else once + piece
                twice = once if twice is None else twice + once
                thrice = twice if thrice is None else thrice + twice
            at = pl.ds(first + 8 * v, 8)
            sums[at, :LANES] = once
            sums[at, LANES : 2 * LANES] = twice
            sums[at, 2 * LANES :] = thrice

    def both(step, entry):
        for n in range(UNROLL):
            entry(step * UNROLL + n)

    lax.fori_loop(0, LIST // UNROLL, lambda step, u: (both(step, forward), u)[1], 0)
    image_ref[0, 0] = dot(feats_t[...], weights_b[...]).T.astype(bf16)
    lax.fori_loop(
        0, LIST // UNROLL, lambda step, u: (both(step, lambda n: backward(LIST - 1 - n)), u)[1], 0
    )

    pulled = dot(weights_b[...], grad_ref[0, 0]).astype(bf16)
    high = sums[...].astype(bf16)
    middle = (sums[...] - high.astype(f32)).astype(bf16)
    table = dot(moments[...], high, NT) + dot(moments[...], middle, NT)
    s, sx, sy, sxx, sxy, syy, t, tx, ty, w = (table[n : n + 1] for n in range(10))
    m0, mx, mxx = s, sx, sxx
    my = sy + 16.0 * s - 4.0 * t
    mxy = sxy + 16.0 * sx - 4.0 * tx
    myy = syy + 32.0 * sy + 256.0 * s - 8.0 * ty - 144.0 * t + 32.0 * w
    dx, dy = mx - cx * m0, my - cy * m0
    dxx = mxx - 2.0 * cx * mx + cx * cx * m0
    dxy = mxy - cx * my - cy * mx + cx * cy * m0
    dyy = myy - 2.0 * cy * my + cy * cy * m0
    grads = jnp.concatenate(
        [
            a * dx + b * dy,
            b * dx + c * dy,
            -0.5 * (a * dxx + b * dxy),
            -0.5 * (c * dyy + b * dxy),
            -root * dxy,
            m0 / (1.0 + jnp.exp(logit)),
            jnp.zeros((2, EVERY), f32),
        ],
        axis=0,
    )
    high = grads.astype(bf16).astype(f32)
    low = grads - high
    group = iota((8, LANES), 1) // 32
    for k in range(LIST):
        pair = [part[:, BLOCK * k : BLOCK * (k + 1)] for part in (high, low)]
        pair = [jnp.where(group == i, part, 0.0) for part in pair for i in range(4)]
        pair.append(jnp.zeros((LANES - 64, LANES), f32))
        turned = jnp.concatenate(pair, axis=0).T
        packed = turned[0:32] + turned[32:64] + turned[64:96] + turned[96:128]
        at = pl.multiple_of((tile * LIST + k) * slices, slices)
        for i in range(4):
            first = BLOCK * k + 32 * i
            back[pl.ds(at, slices), F * i : F * (i + 1)] = pulled[first : first + 32]
        back[pl.ds(at, slices), 4 * F :] = packed.astype(bf16)

    @pl.when(tile == 1)
    def _():
        sent_ref[...] = dot(perm[...], back[...], TN).astype(bf16)


def finish_kernel(slab_ref, centers_ref, scales_ref, corr_ref, opac_ref, feats_ref, wide, small, tall):
    slices, held = slab_ref.shape[0], HELD
    for n in range(slices):
        for i in range(4):
            wide[i, held * n : held * (n + 1), :] = slab_ref[
                n, held * i : held * (i + 1), :
            ].astype(f32)
        small[8 * n : 8 * n + 8, :] = slab_ref[n, 4 * held :, :].astype(f32)
    lane = iota((slices, LANES), 1)
    for n in range(held):
        at = pl.ds(n, slices, stride=held)
        packed = small[pl.ds(n % 6, slices, stride=8), :]
        for i in range(4):
            feats_ref[n, pl.ds(i, slices, stride=4), :] = wide[i, at, :]
            tall[pl.ds(BLOCK * n + i, slices, stride=4), :] = jnp.where(
                lane // 8 == 4 * (n // 6) + i, packed, 0.0
            )
    rank = jnp.where(iota((8, LANES), 1) % 8 == iota((8, LANES), 0), 1.0, 0.0).astype(bf16)
    table = dot(rank, tall[...].astype(bf16), NT)
    for n in range(held):
        own = table[:, BLOCK * n : BLOCK * (n + 1)]
        centers_ref[n] = own[0:2]
        scales_ref[n] = own[2:4]
        corr_ref[n : n + 1, :] = own[4:5]
        opac_ref[n : n + 1, :] = own[5:6]


def cut_kernel(view_ref, centers_ref, scales_ref, corr_ref, opac_ref, feats_ref, out_ref, pairs):
    held = feats_ref.shape[0]
    view = view_ref[0]
    part = 4
    base = pl.multiple_of((view // 4) * 16, 16)
    near = feats_ref[:, pl.ds(base, 16), :].reshape(held * 16, F)
    row, column = iota((held, held * 16), 0), iota((held, held * 16), 1)
    cuts = []
    for i in range(part):
        hot = jnp.where(column == row * 16 + (view % 4) * part + i, 1.0, 0.0).astype(bf16)
        cuts.append(dot(hot, near))
    for n in range(held):
        pairs[0, 2 * n : 2 * n + 2, :] = centers_ref[n].astype(f32)
        pairs[1, 2 * n : 2 * n + 2, :] = scales_ref[n].astype(f32)
    row, column = iota((held, 2 * held), 0), iota((held, 2 * held), 1)
    params = []
    for which in range(2):
        for j in range(2):
            hot = jnp.where(column == 2 * row + j, 1.0, 0.0).astype(bf16)
            params.append(dot(hot, pairs[which].astype(bf16)).astype(bf16))
    params += [corr_ref[...], opac_ref[...]]
    gauss, lane = iota((BLOCK, LANES), 0) - view * part, iota((BLOCK, LANES), 1)
    small = jnp.zeros((held, LANES), f32)
    for j, param in enumerate(params):
        chosen = (lane == gauss + part * j) & (gauss >= 0) & (gauss < part)
        small = small + dot(param, jnp.where(chosen, 1.0, 0.0).astype(bf16))
    slab = jnp.concatenate(cuts + [pack_rows(small.astype(bf16))], axis=0).astype(bf16)
    for n in range(out_ref.shape[0]):
        out_ref[n] = slab


def in_vmem(kernel, shape, *args):
    spec = pl.BlockSpec(memory_space=pltpu.VMEM)
    args = [pltpu.with_memory_space_constraint(arg, pltpu.VMEM) for arg in args]
    return pl.pallas_call(
        kernel,
        out_shape=pltpu.VMEM(shape, bf16),
        in_specs=[spec] * len(args),
        out_specs=spec,
    )(*args)


def tile_call(pads, offset, blocks, grad):
    count = blocks.shape[0]
    smem = pl.BlockSpec(memory_space=pltpu.SMEM)
    whole = pl.BlockSpec((count, WIDTH), lambda t: (0, 0))
    image = pl.BlockSpec((1, 1, PIX, F), lambda t: (0, t, 0, 0))
    return pl.pallas_call(
        tile_kernel,
        grid=(2,),
        out_shape=(
            jax.ShapeDtypeStruct(grad.shape, bf16),
            jax.ShapeDtypeStruct((count, WIDTH), bf16),
        ),
        in_specs=[smem, smem, whole, image],
        out_specs=(image, whole),
        scratch_shapes=[
            pltpu.VMEM((count, WIDTH), bf16),
            pltpu.VMEM((count, count), bf16),
            pltpu.VMEM((LANES, PIX), bf16),
            pltpu.VMEM((16, 3 * LANES), bf16),
            pltpu.VMEM((EVERY, F), bf16),
            pltpu.VMEM((F, EVERY), bf16),
            pltpu.VMEM((EVERY, LANES), bf16),
            pltpu.VMEM((EVERY, PIX), f32),
            pltpu.VMEM((EVERY, PIX), bf16),
            pltpu.VMEM((EVERY, PIX), f32),
            pltpu.VMEM((BLOCK, PIX), f32),
            pltpu.VMEM((EVERY, 3 * LANES), f32),
            pltpu.VMEM((8 * CHUNKS, LANES), f32),
            pltpu.VMEM((8 * CHUNKS, LANES), f32),
            pltpu.VMEM((count, WIDTH), bf16),
        ],
        compiler_params=pltpu.CompilerParams(vmem_limit_bytes=48 * 1024 * 1024),
    )(pads, offset, blocks, grad)


def shards(
    centers,
    log_scales,
    correlation,
    opacity_logit,
    features,
    view_offset,
    block_list,
    pad_count,
    block_home,
    image_grad,
):
    views, tiles = lax.axis_size("view"), lax.axis_size("tile")
    held = centers.shape[0]
    total = held * tiles
    view = lax.axis_index("view")

    def exchange(x, axis):
        return lax.all_to_all(x, axis, split_axis=0, concat_axis=0, tiled=True)

    spec = pl.BlockSpec(memory_space=pltpu.VMEM)
    slab = pl.pallas_call(
        cut_kernel,
        out_shape=pltpu.VMEM((tiles, SENT, LANES), bf16),
        in_specs=[pl.BlockSpec(memory_space=pltpu.SMEM)] + [spec] * 5,
        out_specs=spec,
        scratch_shapes=[pltpu.VMEM((2, 2 * held, LANES), f32)],
    )(view.reshape(1), centers, log_scales, correlation, opacity_logit, features)
    table = exchange(slab, "tile")
    rows = jnp.take(block_home, block_list.reshape(-1))
    slots = rows.shape[0]
    asked = lax.all_gather(rows.reshape(1, 1, slots), "view", tiled=True)
    wanted, ids = pl.pallas_call(
        gather_kernel,
        out_shape=(
            pltpu.VMEM((views * slots, WIDTH), bf16), pltpu.VMEM((1, views * slots), jnp.int32)
        ),
        in_specs=[spec] * 2,
        out_specs=(spec,) * 2,
        scratch_shapes=[
            pltpu.VMEM((views, slots), jnp.int32), pltpu.VMEM((total, WIDTH), f32)
        ],
    )(*(pltpu.with_memory_space_constraint(x, pltpu.VMEM) for x in (asked, table)))
    blocks = exchange(wanted, "view")

    image, sent = tile_call(pad_count, view_offset, blocks, image_grad)

    came = exchange(sent, "view")
    partial = in_vmem(scatter_kernel, (tiles, SENT, LANES), ids, came)
    partial = exchange(partial, "tile")
    slab = in_vmem(sum_kernel, (views, SENT, LANES), partial)
    slab = exchange(slab, "view")

    shape = lambda *dims: jax.ShapeDtypeStruct(dims, f32)
    spec = pl.BlockSpec(memory_space=pltpu.VMEM)
    grads = pl.pallas_call(
        finish_kernel,
        out_shape=(
            shape(held, 2, BLOCK), shape(held, 2, BLOCK), shape(held, BLOCK), shape(held, BLOCK),
            shape(held, BLOCK, F),
        ),
        in_specs=[spec],
        out_specs=(spec,) * 5,
        scratch_shapes=[
            pltpu.VMEM((4, views * held, LANES), f32),
            pltpu.VMEM((views * 8, LANES), f32),
            pltpu.VMEM((held * BLOCK, LANES), f32),
        ],
    )(pltpu.with_memory_space_constraint(slab, pltpu.VMEM))
    return (image, *grads)


def solution(mesh):
    in_specs = (
        P("tile", None, None),
        P("tile", None, None),
        P("tile", None),
        P("tile", None),
        P("tile", None, None),
        P("view", None),
        P("view", "tile", None),
        P("view", "tile"),
        P(),
        P("view", "tile", None, None),
    )
    out_specs = (
        P("view", "tile", None, None),
        P("tile", None, None),
        P("tile", None, None),
        P("tile", None),
        P("tile", None),
        P("tile", None, None),
    )
    return jax.shard_map(shards, mesh=mesh, in_specs=in_specs, out_specs=out_specs, check_vma=False)
```
